32 devices in a mesh: gx: 4 (over y, core), gy: 2 (over x), gz: 4 (over z).
Axes of the slice: x: 2, y: 2, z: 4, core: 2. Of those that a mesh axis runs over, the one named last changes fastest.
Arguments:
- charges: float32 [64, 64, 512], P('gx', 'gy', 'gz'), may hold values from -6 to 6
- term_width: float32 [2, 4], replicated, may hold values from 0.8 to 3.5
- term_weight: float32 [2, 4], replicated, may hold values from 0.5 to 2
Outputs:
- potential: float32 [64, 64, 512], P('gx', 'gy', 'gz')
The draws below stay inside these ranges and needn't reach their ends.
All inputs are finite; a program needn't handle non-finite values.
Results may differ from the reference program's by a relative error of at most 0.00025.
Values sent between devices are 32-bit elements; how exact they have to be, the bound alone decides.
A program may use at most 64 MiB of HBM per device.

```python
import math
import jax
import jax.numpy as jnp
from jax import lax

TERMS = 4
RADIUS = 8
NX = 64
NY = 64
NZ = 512


def draw_charges(key, part):
    return jnp.clip(jax.random.normal(key, (NX, NY, NZ), jnp.float32), -6.0, 6.0)


def setup_inputs(seed: int = 0) -> dict:
    seeds = jax.random.split(jax.random.key(seed), 4)
    charges = draw_charges(jax.random.fold_in(seeds[3], 71), 0)
    term_width = jnp.clip(jnp.exp(jax.random.uniform(seeds[1], (2, TERMS), jnp.float32, math.log(0.8), math.log(3.5))), 0.8, 3.5)
    term_weight = jnp.clip(jax.random.uniform(seeds[2], (2, TERMS), jnp.float32, 0.5, 2.0), 0.5, 2.0)
    return {"charges": charges, "term_width": term_width, "term_weight": term_weight}


screening = 0.01
strength = 4.0


def gaussian_taps(widths):
    offsets = jnp.arange(-RADIUS, RADIUS + 1).astype(widths.dtype)
    values = jnp.exp(-(offsets[None, :] ** 2) / (2.0 * widths[:, None] ** 2))
    return values / jnp.sum(values, axis=1, keepdims=True)


def convolve(padded, taps, axis, length):
    total = taps[0] * lax.slice_in_dim(padded, 0, length, axis=axis)
    for offset in range(1, 2 * RADIUS + 1):
        total = total + taps[offset] * lax.slice_in_dim(padded, offset, offset + length, axis=axis)
    return total


def smooth_level(field, widths, weights):
    taps = gaussian_taps(widths)
    padded = jnp.pad(field, RADIUS, mode="wrap")
    shape = field.shape
    result = None
    for term_index in range(TERMS):
        first_pass = convolve(padded, taps[term_index], 0, shape[0])
        second_pass = convolve(first_pass, taps[term_index], 1, shape[1])
        third_pass = convolve(second_pass, taps[term_index], 2, shape[2])
        contrib = weights[term_index] * third_pass
        result = contrib if result is None else result + contrib
    return result


def restrict(field):
    shape = field.shape
    return field.reshape(shape[0] // 2, 2, shape[1] // 2, 2, shape[2] // 2, 2).mean(axis=(1, 3, 5))


def expand(field):
    return jnp.repeat(jnp.repeat(jnp.repeat(field, 2, axis=0), 2, axis=1), 2, axis=2)


def axis_lam(count, dtype):
    modes = jnp.arange(count).astype(dtype)
    return 2.0 - 2.0 * jnp.cos((2.0 * math.pi / count) * modes)


def solve_top(coarse):
    shape = coarse.shape
    lam = axis_lam(shape[0], coarse.dtype)[:, None, None] + axis_lam(shape[1], coarse.dtype)[None, :, None] + axis_lam(shape[2], coarse.dtype)[None, None, :]
    zeroed = lam <= 0.0
    mult = jnp.where(zeroed, 0.0, strength * jnp.exp(-lam) / (lam + screening))
    spectrum = jnp.fft.fftn(coarse) * mult
    return jnp.real(jnp.fft.ifftn(spectrum)).astype(coarse.dtype)


def reference(charges, term_width, term_weight):
    middle = restrict(charges)
    coarse = restrict(middle)
    near = smooth_level(charges, term_width[0], term_weight[0])
    between = smooth_level(middle, term_width[1], term_weight[1])
    distant = solve_top(coarse)
    return near + expand(between + expand(distant))
```

```python
import functools
import math

import jax
import jax.numpy as jnp
import numpy as np
from jax import lax
from jax.experimental import pallas as pl
from jax.experimental.pallas import tpu as pltpu
from jax.sharding import PartitionSpec as P

TERMS = 4
R = 8
HIGHEST = lax.Precision.HIGHEST
screening = 0.01
strength = 4.0
AXES = ("gx", "gy", "gz")
MESH = pl.DeviceIdType.MESH
F32 = jnp.float32
BF16 = jnp.bfloat16


def real_basis(count):
    points = np.arange(count)
    rows, freqs = [], []
    for m in range(count // 2 + 1):
        angle = 2.0 * np.pi * ((m * points) % count) / count
        single = m == 0 or 2 * m == count
        scale = math.sqrt((1.0 if single else 2.0) / count)
        rows.append(scale * np.cos(angle))
        freqs.append(m)
        if not single:
            rows.append(scale * np.sin(angle))
            freqs.append(m)
    return np.stack(rows), np.array(freqs)


def lam_of(freqs, count):
    return 2.0 - 2.0 * np.cos(2.0 * np.pi * freqs / count)


def top_tables(sizes, block):
    ngx, ngy, ngz = sizes
    cx, cy, cz = block
    nx, ny, nz = ngx * cx, ngy * cy, ngz * cz
    (qx, fx), (qy, fy), (qz, fz) = real_basis(nx), real_basis(ny), real_basis(nz)
    lam = (
        lam_of(fx, nx)[:, None, None] + lam_of(fy, ny)[None, :, None] + lam_of(fz, nz)[None, None, :]
    )
    zero = (fx[:, None, None] + fy[None, :, None] + fz[None, None, :]) == 0
    mult = np.where(zero, 0.0, strength * np.exp(-lam) / (lam + screening)).reshape(nx * ny, nz)
    kron = np.kron(qx, qy).reshape(nx * ny, ngx, cx, ngy, cy)
    forward = kron.transpose(0, 2, 1, 3, 4).reshape(nx * ny, nx * ny)
    inverse = kron.transpose(1, 3, 2, 4, 0).reshape(ngx * ngy, cx * cy, nx * ny)
    spread = np.repeat(qz, 4, axis=1).reshape(nz, ngz, 4 * cz).transpose(1, 0, 2)
    return [np.asarray(t, np.float32) for t in (qz.T, forward, mult, inverse, spread)]


def split(value):
    high = value.astype(BF16)
    return high, (value - high.astype(F32)).astype(BF16)


NN = (((1,), (0,)), ((), ()))
NT = (((1,), (1,)), ((), ()))


def mm(a, b, dims=NN):
    return lax.dot_general(a, b, dims, preferred_element_type=F32)


def dot3(a, b, dims=NN):
    (ah, al), (bh, bl) = a, b
    return mm(ah, bh, dims) + (mm(al, bh, dims) + mm(ah, bl, dims))


def dot2(a, exact):
    return mm(a[0], exact) + mm(a[1], exact)


def iota(shape, dim):
    return lax.broadcasted_iota(jnp.int32, shape, dim)


def body(sizes, block, fused, *refs):
    ngx, ngy, ngz = sizes
    bx, by, bz = block
    mx, my, mz = bx // 2, by // 2, bz // 2
    cx, cy, cz = bx // 4, by // 4, bz // 4
    count = ngx * ngy * ngz
    if fused:
        (charges, width, weight, qz_h, fwd_h, mult_h, inv_h, spr_h, out) = refs[:9]
        refs = refs[9:]
    else:
        (charges, width, weight, out) = refs[:4]
        refs = refs[4:]
    (fe, x1, ph, pl_, me_, m1, mh, ml, ze, zr, t_hi, t_lo, taps, bet, up, dis, ssem, rsem, lsem) = refs[:19]
    if fused:
        (ga, qz_v, fwd_v, mult_v, inv_v, spr_v, gs, gr) = refs[19:]

    ix, iy, iz = (lax.axis_index(a) for a in AXES)
    index = (ix * ngy + iy) * ngz + iz

    def step(axis, by_):
        position = [ix, iy, iz]
        n = sizes[axis]
        position[axis] = lax.rem(position[axis] + by_ + n, n)
        return tuple(position)

    def coords(i):
        return (i // (ngy * ngz), (i // ngz) % ngy, i % ngz)

    barrier = pltpu.get_barrier_semaphore()
    if fused:
        @pl.loop(1, count)
        def _(d):
            pl.semaphore_signal(
                barrier, 1, device_id=coords((index + d) % count), device_id_type=MESH
            )
        greetings = count - 1
    else:
        greetings = 0
        for axis in range(3):
            for by_ in (1, -1) if sizes[axis] > 2 else (1,):
                pl.semaphore_signal(barrier, 1, device_id=step(axis, by_), device_id_type=MESH)
                greetings += 1

    local = [pltpu.make_async_copy(charges, fe.at[R:R + bx, R:R + by], lsem.at[0])]
    if fused:
        local += [
            pltpu.make_async_copy(qz_h, qz_v, lsem.at[1]),
            pltpu.make_async_copy(fwd_h, fwd_v, lsem.at[2]),
            pltpu.make_async_copy(mult_h, mult_v, lsem.at[3]),
            pltpu.make_async_copy(inv_h.at[ix * ngy + iy], inv_v, lsem.at[4]),
            pltpu.make_async_copy(spr_h.at[iz], spr_v, lsem.at[5]),
        ]
    for copy in local:
        copy.start()

    def remote(src, dst, slot, target):
        return pltpu.make_async_remote_copy(
            src_ref=src, dst_ref=dst, send_sem=ssem.at[slot], recv_sem=rsem.at[slot],
            device_id=target, device_id_type=MESH,
        )

    xp, xm, yp, ym, zp, zm = step(0, 1), step(0, -1), step(1, 1), step(1, -1), step(2, 1), step(2, -1)
    lo_x, hi_x, lo_y, hi_y = slice(0, R), slice(R + bx, 2 * R + bx), slice(0, R), slice(R + by, 2 * R + by)
    own_x, own_y = slice(R, R + bx), slice(R, R + by)
    x_halo = [
        remote(charges.at[bx - R:bx], fe.at[lo_x, own_y], 0, xp),
        remote(charges.at[0:R], fe.at[hi_x, own_y], 1, xm),
    ]
    y_halo = [
        remote(charges.at[:, by - R:by], fe.at[own_x, lo_y], 2, yp),
        remote(charges.at[:, 0:R], fe.at[own_x, hi_y], 3, ym),
    ]
    corner = [
        remote(fe.at[bx:bx + R, lo_y], fe.at[lo_x, lo_y], 4, xp),
        remote(fe.at[bx:bx + R, hi_y], fe.at[lo_x, hi_y], 5, xp),
        remote(fe.at[R:2 * R, lo_y], fe.at[hi_x, lo_y], 6, xm),
        remote(fe.at[R:2 * R, hi_y], fe.at[hi_x, hi_y], 7, xm),
    ]
    mown, mlo, mhi = slice(R, R + mx), slice(0, R), slice(R + mx, 2 * R + mx)
    mid_x = [
        remote(me_.at[0, mx:R + mx], me_.at[0, mlo], 8, xp),
        remote(me_.at[0, R:2 * R], me_.at[0, mhi], 9, xm),
    ]
    mid_y = [remote(me_.at[0, mown], me_.at[1, mown], 10, yp)]
    mid_c = [
        remote(me_.at[0, mlo], me_.at[1, mlo], 12, yp),
        remote(me_.at[0, mhi], me_.at[1, mhi], 13, yp),
    ]
    high = 1
    if ngy > 2:
        high = 2
        mid_y.append(remote(me_.at[0, mown], me_.at[2, mown], 11, ym))
        mid_c.append(remote(me_.at[0, mlo], me_.at[2, mlo], 14, ym))
        mid_c.append(remote(me_.at[0, mhi], me_.at[2, mhi], 15, ym))
    z_edge = [
        remote(ze.at[0:R], zr.at[0:R], 16, zm),
        remote(ze.at[R:2 * R], zr.at[R:2 * R], 17, zp),
    ]

    pl.semaphore_wait(barrier, greetings)
    for copy in y_halo + x_halo:
        copy.start()

    weights_edge = []
    for level in range(2):
        edges = []
        for k in range(TERMS):
            sigma = jnp.full((1, 128), width[level, k], F32)
            rate = 1.0 / (2.0 * sigma * sigma)
            values = [jnp.exp(-(float(t * t) * rate)) for t in range(R + 1)]
            total = values[0]
            for t in range(1, R + 1):
                total = total + 2.0 * values[t]
            inverse = 1.0 / total
            for t in range(R + 1):
                taps[level * TERMS + k, t] = jnp.broadcast_to(values[t] * inverse, (8, 128))
            scale = inverse * weight[level, k]

            def band(d, keep):
                d = d.astype(F32)
                inside = jnp.abs(d) <= float(R)
                if keep is not None:
                    inside = jnp.logical_and(inside, keep)
                return jnp.where(inside, jnp.exp(-(d * d * rate)) * scale, 0.0)

            if level == 0:
                shape = (bz, bz)
                hi, lo = split(band(iota(shape, 0) - iota(shape, 1), None))
                t_hi[0, k * bz:(k + 1) * bz] = hi
                t_lo[0, k * bz:(k + 1) * bz] = lo
                shape = (2 * R, bz)
                row, z = iota(shape, 0), iota(shape, 1)
                edges.append(band(z - jnp.where(row < R, row - R, row - R + bz), None))
            else:
                shape = (bz, bz)
                row = iota(shape, 0)
                for half in range(2):
                    keep = jnp.right_shift(row, mz.bit_length() - 1) == half
                    hi, lo = split(band((row - half * mz) - jnp.right_shift(iota(shape, 1), 1), keep))
                    t_hi[1 + half, k * bz:(k + 1) * bz] = hi
                    t_lo[1 + half, k * bz:(k + 1) * bz] = lo
                shape = (2 * R, bz)
                row, z = iota(shape, 0), iota(shape, 1)
                target = jnp.where(row < R, row - R, row - R + mz)
                pair = [
                    band(z - half * mz - target, jnp.right_shift(z, mz.bit_length() - 1) == half)
                    for half in range(2)
                ]
                edges.append(jnp.concatenate(pair, axis=0))
        weights_edge.append(split(jnp.concatenate(edges, axis=1)))

    local[0].wait()
    halves = []
    for half in range(2):
        rows = []
        for i in range(mx):
            total = None
            for a in range(2):
                for b in range(2):
                    part = fe[R + 2 * i + a, pl.ds(R + half * my + b, R, stride=2), :]
                    total = part if total is None else total + part
            rows.append(total)
        halves.append(jnp.concatenate(rows, axis=0))
    row, col = iota((2 * bz, bz), 0), iota((2 * bz, bz), 1)
    pool = jnp.where(jnp.right_shift(row, 1) == col, 0.125, 0.0).astype(BF16)
    middle = dot2(split(jnp.concatenate(halves, axis=1)), pool)
    me_[0, mown] = middle.reshape(mx, R, bz)
    if fused:
        lanes = []
        for i in range(cx):
            total = None
            for a in range(4):
                for b in range(4):
                    part = fe[R + 4 * i + a, pl.ds(R + b, cy, stride=4), :]
                    total = part if total is None else total + part
            lanes.append(total)
        row, col = iota((cx * bz, bz), 0), iota((cx * bz, bz), 1)
        pool = jnp.where(jnp.right_shift(row, 2) == col, 1.0 / 64.0, 0.0).astype(BF16)
        ga[ix * ngy + iy, iz] = dot2(split(jnp.concatenate(lanes, axis=1)), pool)
    for copy in mid_x + mid_y:
        copy.start()

    def gather_copy(source, target, d):
        tile = ga.at[source // ngz, source % ngz]
        return pltpu.make_async_remote_copy(
            src_ref=tile, dst_ref=tile, send_sem=gs.at[d], recv_sem=gr.at[source],
            device_id=coords(target), device_id_type=MESH,
        )

    if fused:
        @pl.loop(1, count)
        def _(d):
            gather_copy(index, (index + d) % count, d).start()

    for copy in y_halo:
        copy.wait_recv()
    for copy in corner:
        copy.start()

    def taps_of(level, k):
        return [taps[level * TERMS + k, t] for t in range(R + 1)]

    for copy in x_halo:
        copy.wait_recv()

    def x_filter(load, store, level, tiles, length):
        @pl.loop(0, length)
        def _(i):
            g = [taps_of(level, k) for k in range(TERMS)]
            for tile in tiles:
                centre = load(i + R, tile)
                totals = [g[k][0] * centre for k in range(TERMS)]
                for t in range(1, R + 1):
                    pair = load(i + R - t, tile) + load(i + R + t, tile)
                    totals = [totals[k] + g[k][t] * pair for k in range(TERMS)]
                for k in range(TERMS):
                    store(k, i, tile, totals[k])

    def load_f(i, tile):
        return fe[i, tile * 8:tile * 8 + 8, :]

    def store_f(k, i, tile, value):
        x1[k, i, tile * 8:tile * 8 + 8, :] = value

    last = (by + R) // 8
    x_filter(load_f, store_f, 0, range(1, last), bx)

    for copy in mid_x:
        copy.wait_recv()
    for copy in mid_c:
        copy.start()
    for copy in corner:
        copy.wait_recv()
    x_filter(load_f, store_f, 0, (0, last), bx)

    @pl.loop(0, bx)
    def _(i):
        for k in range(TERMS):
            g = taps_of(0, k)
            for pair in range(by // 16):
                base = R + pair * 16
                parts = []
                for s in range(2):
                    at = base + 8 * s
                    total = g[0] * x1[k, i, at:at + 8, :]
                    for t in range(1, R + 1):
                        total = total + g[t] * (
                            x1[k, i, at - t:at - t + 8, :] + x1[k, i, at + t:at + t + 8, :]
                        )
                    parts.append(total)
                hi, lo = split(jnp.concatenate(parts, axis=0))
                rows = pl.ds(pl.multiple_of(i * by + pair * 16, 16), 16)
                ph[rows, k * bz:(k + 1) * bz] = hi
                pl_[rows, k * bz:(k + 1) * bz] = lo

    for copy in mid_y + mid_c:
        copy.wait_recv()
    slots = range(high + 1)

    def load_m(i, slot):
        return me_[slot, i]

    def store_m(k, i, slot, value):
        m1[slot, k, i] = value

    x_filter(load_m, store_m, 1, slots, mx)
    low_lanes = iota((R, bz), 1) < mz

    @pl.loop(0, mx // 2)
    def _(i):
        for k in range(TERMS):
            g = taps_of(1, k)
            parts = []
            for s in range(2):
                own, low, top_ = m1[0, k, 2 * i + s], m1[1, k, 2 * i + s], m1[high, k, 2 * i + s]
                bet[s, 0:8] = pltpu.roll(jnp.where(low_lanes, own, low), mz, 1)
                bet[s, 8:16] = own
                bet[s, 16:24] = pltpu.roll(jnp.where(low_lanes, top_, own), mz, 1)
                total = g[0] * own
                for t in range(1, R + 1):
                    total = total + g[t] * (bet[s, 8 - t:16 - t, :] + bet[s, 8 + t:16 + t, :])
                parts.append(total)
            hi, lo = split(jnp.concatenate(parts, axis=0))
            rows = pl.ds(pl.multiple_of(i * 16, 16), 16)
            mh[rows, k * bz:(k + 1) * bz] = hi
            ml[rows, k * bz:(k + 1) * bz] = lo

    fine = (ph[...], pl_[...])
    mid = (mh[...], ml[...])
    ze[:, 0:bx * by] = dot3(weights_edge[0], fine, NT)
    edge = dot3(weights_edge[1], mid, NT)
    ze[:, bx * by:] = jnp.concatenate([edge[0:2 * R], edge[2 * R:4 * R]], axis=1)
    for copy in z_edge:
        copy.start()

    near = dot3(fine, (t_hi[0], t_lo[0]))
    out[...] = near.reshape(bx, by, bz)
    between = [dot3(mid, (t_hi[1 + half], t_lo[1 + half])) for half in range(2)]

    if fused:
        for copy in local[1:]:
            copy.wait()

        @pl.loop(1, count)
        def _(d):
            gather_copy((index - d + count) % count, index, d).wait_recv()

        group = jnp.right_shift(iota((ngx * ngy * cy, bz), 1), cz.bit_length() - 1)
        blocks = [ga[:, j].reshape(ngx * ngy * cy, bz) for j in range(ngz)]
        lines = []
        for i in range(cx):
            line = None
            for j in range(ngz):
                shift = (j * cz - i * cz) % bz
                moved = pltpu.roll(blocks[j], shift, 1) if shift else blocks[j]
                line = moved if line is None else jnp.where(group == j, moved, line)
            lines.append(line)
        lines = jnp.concatenate(lines, axis=0)
        modes = dot3(split(lines), split(qz_v[...]))
        modes = dot3(split(fwd_v[...]), split(modes)) * mult_v[...]
        modes = dot3(split(inv_v[...]), split(modes))
        distant = dot3(split(modes), split(spr_v[...]))
        for i in range(cx):
            part = distant[i * cy:(i + 1) * cy]
            dis[i, pl.ds(0, cy, stride=2), :] = part
            dis[i, pl.ds(1, cy, stride=2), :] = part

    for copy in z_edge:
        copy.wait_recv()
    row, col = iota((2 * R, bz), 0), iota((2 * R, bz), 1)
    place = jnp.where(row < R, row + bz - R, row - R) == col
    place = jnp.where(place, 1.0, 0.0).astype(BF16)
    spread = jnp.where(row < R, row + mz - R, row - R) == jnp.right_shift(col, 1)
    spread = jnp.where(spread, 1.0, 0.0).astype(BF16)
    edge = dot2(split(zr[:, bx * by:].T), spread)
    for half in range(2):
        for i in range(mx):
            at = i * R
            value = between[half][at:at + R] + edge[half * mx * R + at:half * mx * R + at + R]
            if fused:
                value = value + dis[i // 2, half * R:half * R + R, :]
            up[i, pl.ds(2 * R * half, R, stride=2), :] = value
            up[i, pl.ds(2 * R * half + 1, R, stride=2), :] = value
    edge = dot2(split(zr[:, 0:bx * by].T), place)
    for i in range(bx):
        out[i] = out[i] + (edge[i * by:(i + 1) * by] + up[i // 2])

    for copy in x_halo + y_halo + corner + mid_x + mid_y + mid_c + z_edge:
        copy.wait_send()
    if fused:
        @pl.loop(1, count)
        def _(d):
            gather_copy(index, (index + d) % count, d).wait_send()


def expand(field):
    return jnp.repeat(jnp.repeat(jnp.repeat(field, 2, axis=0), 2, axis=1), 2, axis=2)


def coarse_of(field):
    s = field.shape
    return field.reshape(s[0] // 4, 4, s[1] // 4, 4, s[2] // 4, 4).mean(axis=(1, 3, 5))


def turn(real, imag, cosine, sine, form, sign):
    ein = functools.partial(jnp.einsum, form, precision=HIGHEST)
    return (
        ein(cosine, real) + sign * ein(sine, imag),
        ein(cosine, imag) - sign * ein(sine, real),
    )


def dft(count):
    modes = np.arange(count)
    angle = 2.0 * np.pi * (modes[:, None] * modes[None, :] % count) / count
    return jnp.asarray(np.cos(angle), F32), jnp.asarray(np.sin(angle), F32)


def solve_top(coarse, sizes):
    bx, by, bz = coarse.shape
    nx, ny, nz = bx * sizes[0], by * sizes[1], bz * sizes[2]
    a2a = functools.partial(lax.all_to_all, tiled=True)
    column = lax.all_gather(coarse, "gx", axis=0, tiled=True)
    tx, ty, tz = dft(nx), dft(ny), dft(nz)
    real, imag = turn(column, jnp.zeros_like(column), *tx, "mx,xyz->myz", 1.0)
    pencil = a2a(jnp.stack([real, imag]), "gy", split_axis=1, concat_axis=2)
    pencil = a2a(pencil, "gz", split_axis=1, concat_axis=3)
    real, imag = turn(pencil[0], pencil[1], *ty, "my,xyz->xmz", 1.0)
    real, imag = turn(real, imag, *tz, "mz,xyz->xym", 1.0)
    rows_y = nx // sizes[1]
    rows = rows_y // sizes[2]
    start = lax.axis_index("gy") * rows_y + lax.axis_index("gz") * rows
    lam_x = jnp.asarray(lam_of(np.arange(nx), nx), F32)
    lam = (
        lax.dynamic_slice_in_dim(lam_x, start, rows, 0)[:, None, None]
        + jnp.asarray(lam_of(np.arange(ny), ny), F32)[None, :, None]
        + jnp.asarray(lam_of(np.arange(nz), nz), F32)[None, None, :]
    )
    mult = jnp.where(lam <= 0.0, 0.0, strength * jnp.exp(-lam) / (lam + screening))
    real, imag = turn(real * mult, imag * mult, *tz, "mz,xyz->xym", -1.0)
    back = a2a(jnp.stack([real, imag]), "gz", split_axis=3, concat_axis=1)
    real, imag = turn(back[0], back[1], *ty, "my,xyz->xmz", -1.0)
    back = a2a(jnp.stack([real, imag]), "gy", split_axis=2, concat_axis=1)
    whole, _ = turn(back[0], back[1], *tx, "mx,xyz->myz", -1.0)
    whole = whole / float(nx * ny * nz)
    return lax.dynamic_slice_in_dim(whole, lax.axis_index("gx") * bx, bx, 0)


def shards(sizes, charges, width, weight):
    bx, by, bz = block = charges.shape
    mx, my = bx // 2, by // 2
    cx, cy, cz = coarse = (bx // 4, by // 4, bz // 4)
    ngx, ngy, ngz = sizes
    count = ngx * ngy * ngz
    points = ngx * cx * ngy * cy
    fused = points <= 512 and ngz * cz == bz and count <= 64
    vmem = pltpu.VMEM
    slots = 2 if ngy == 2 else 3
    scratch = [
        vmem((bx + 2 * R, by + 2 * R, bz), F32),
        vmem((TERMS, bx, by + 2 * R, bz), F32),
        vmem((bx * by, TERMS * bz), BF16),
        vmem((bx * by, TERMS * bz), BF16),
        vmem((slots, mx + 2 * R, R, bz), F32),
        vmem((slots, TERMS, mx, R, bz), F32),
        vmem((mx * R, TERMS * bz), BF16),
        vmem((mx * R, TERMS * bz), BF16),
        vmem((2 * R, bx * by + 2 * mx * R), F32),
        vmem((2 * R, bx * by + 2 * mx * R), F32),
        vmem((3, TERMS * bz, bz), BF16),
        vmem((3, TERMS * bz, bz), BF16),
        vmem((2 * TERMS, R + 1, 8, 128), F32),
        vmem((2, 3 * R, bz), F32),
        vmem((mx, by, bz), F32),
        vmem((cx, my, bz), F32),
        pltpu.SemaphoreType.DMA((18,)),
        pltpu.SemaphoreType.DMA((18,)),
        pltpu.SemaphoreType.DMA((6,)),
    ]
    operands = [charges, width, weight]
    anywhere = pl.BlockSpec(memory_space=pl.ANY)
    small = pl.BlockSpec(memory_space=pltpu.SMEM)
    specs = [anywhere, small, small]
    if fused:
        tables = top_tables(sizes, coarse)
        operands += [jnp.asarray(t) for t in tables]
        specs += [anywhere] * len(tables)
        scratch += [
            vmem((ngx * ngy, ngz, cy, cx * cz), F32),
            vmem(tables[0].shape, F32),
            vmem(tables[1].shape, F32),
            vmem(tables[2].shape, F32),
            vmem(tables[3].shape[1:], F32),
            vmem(tables[4].shape[1:], F32),
            pltpu.SemaphoreType.DMA((count,)),
            pltpu.SemaphoreType.DMA((count,)),
        ]
    result = pl.pallas_call(
        functools.partial(body, sizes, block, fused),
        out_shape=jax.ShapeDtypeStruct(block, F32),
        in_specs=specs,
        out_specs=pl.BlockSpec(memory_space=pltpu.VMEM),
        scratch_shapes=scratch,
        compiler_params=pltpu.CompilerParams(collective_id=0, has_side_effects=True),
    )(*operands)
    if not fused:
        result = result + expand(expand(solve_top(coarse_of(charges), sizes)))
    return result


def solution(mesh):
    sizes = tuple(mesh.shape[a] for a in AXES)
    placed = (P(*AXES), P(), P())
    return jax.shard_map(
        functools.partial(shards, sizes), mesh=mesh, in_specs=placed, out_specs=P(*AXES),
        check_vma=False,
    )
```

```python
import functools
import math

import jax
import jax.numpy as jnp
import numpy as np
from jax import lax
from jax.experimental import pallas as pl
from jax.experimental.pallas import tpu as pltpu
from jax.sharding import PartitionSpec as P

TERMS = 4
R = 8
HIGHEST = lax.Precision.HIGHEST
screening = 0.01
strength = 4.0
AXES = ("gx", "gy", "gz")
MESH = pl.DeviceIdType.MESH
F32 = jnp.float32
BF16 = jnp.bfloat16


def real_basis(count):
    points = np.arange(count)
    rows, freqs = [], []
    for m in range(count // 2 + 1):
        angle = 2.0 * np.pi * ((m * points) % count) / count
        single = m == 0 or 2 * m == count
        scale = math.sqrt((1.0 if single else 2.0) / count)
        rows.append(scale * np.cos(angle))
        freqs.append(m)
        if not single:
            rows.append(scale * np.sin(angle))
            freqs.append(m)
    return np.stack(rows), np.array(freqs)


def lam_of(freqs, count):
    return 2.0 - 2.0 * np.cos(2.0 * np.pi * freqs / count)


def top_tables(sizes, block):
    ngx, ngy, ngz = sizes
    cx, cy, cz = block
    nx, ny, nz = ngx * cx, ngy * cy, ngz * cz
    (qx, fx), (qy, fy), (qz, fz) = real_basis(nx), real_basis(ny), real_basis(nz)
    lam = (
        lam_of(fx, nx)[:, None, None] + lam_of(fy, ny)[None, :, None] + lam_of(fz, nz)[None, None, :]
    )
    zero = (fx[:, None, None] + fy[None, :, None] + fz[None, None, :]) == 0
    mult = np.where(zero, 0.0, strength * np.exp(-lam) / (lam + screening)).reshape(nx * ny, nz)
    kron = np.kron(qx, qy).reshape(nx * ny, ngx, cx, ngy, cy)
    forward = kron.transpose(0, 2, 3, 1, 4).reshape(nx * ny, nx * ny)
    inverse = kron.transpose(1, 3, 2, 4, 0).reshape(ngx * ngy, cx * cy, nx * ny)
    spread = np.repeat(qz, 4, axis=1).reshape(nz, ngz, 4 * cz).transpose(1, 0, 2)
    return [np.asarray(t, np.float32) for t in (qz.T, forward, mult, inverse, spread)]


def split(value):
    high = value.astype(BF16)
    return high, (value - high.astype(F32)).astype(BF16)


NN = (((1,), (0,)), ((), ()))
NT = (((1,), (1,)), ((), ()))


def mm(a, b, dims=NN):
    return lax.dot_general(a, b, dims, preferred_element_type=F32)


def dot3(a, b, dims=NN):
    (ah, al), (bh, bl) = a, b
    return mm(ah, bh, dims) + (mm(al, bh, dims) + mm(ah, bl, dims))


def dot2(a, exact):
    return mm(a[0], exact) + mm(a[1], exact)


def iota(shape, dim):
    return lax.broadcasted_iota(jnp.int32, shape, dim)


def body(sizes, block, fused, *refs):
    ngx, ngy, ngz = sizes
    bx, by, bz = block
    mx, my, mz = bx // 2, by // 2, bz // 2
    cx, cy, cz = bx // 4, by // 4, bz // 4
    if fused:
        (charges, width, weight, qz_h, fwd_h, mult_h, inv_h, spr_h, out) = refs[:9]
        refs = refs[9:]
    else:
        (charges, width, weight, out) = refs[:4]
        refs = refs[4:]
    (fe, x1, ph, pl_, me_, m1, mh, ml, ze, zr, t_hi, t_lo, taps, bet, up, dis, ssem, rsem, lsem) = refs[:19]
    if fused:
        (ga, qz_v, fwd_v, mult_v, inv_v, spr_v, gs, gr) = refs[19:]

    ix, iy, iz = (lax.axis_index(a) for a in AXES)

    def step(axis, by_):
        position = [ix, iy, iz]
        n = sizes[axis]
        position[axis] = lax.rem(position[axis] + by_ + n, n)
        return tuple(position)

    barrier = pltpu.get_barrier_semaphore()
    greetings = 0
    for axis in range(3):
        n = sizes[axis]
        for off in range(1, n) if fused else ((1, -1) if n > 2 else (1,)):
            pl.semaphore_signal(barrier, 1, device_id=step(axis, off), device_id_type=MESH)
            greetings += 1

    local = [pltpu.make_async_copy(charges, fe.at[R:R + bx, R:R + by], lsem.at[0])]
    if fused:
        local += [
            pltpu.make_async_copy(qz_h, qz_v, lsem.at[1]),
            pltpu.make_async_copy(fwd_h, fwd_v, lsem.at[2]),
            pltpu.make_async_copy(mult_h, mult_v, lsem.at[3]),
            pltpu.make_async_copy(inv_h.at[ix * ngy + iy], inv_v, lsem.at[4]),
            pltpu.make_async_copy(spr_h.at[iz], spr_v, lsem.at[5]),
        ]
    for copy in local:
        copy.start()

    def remote(src, dst, slot, target):
        return pltpu.make_async_remote_copy(
            src_ref=src, dst_ref=dst, send_sem=ssem.at[slot], recv_sem=rsem.at[slot],
            device_id=target, device_id_type=MESH,
        )

    xp, xm, yp, ym, zp, zm = step(0, 1), step(0, -1), step(1, 1), step(1, -1), step(2, 1), step(2, -1)
    lo_x, hi_x, lo_y, hi_y = slice(0, R), slice(R + bx, 2 * R + bx), slice(0, R), slice(R + by, 2 * R + by)
    own_x, own_y = slice(R, R + bx), slice(R, R + by)
    x_halo = [
        remote(charges.at[bx - R:bx], fe.at[lo_x, own_y], 0, xp),
        remote(charges.at[0:R], fe.at[hi_x, own_y], 1, xm),
    ]
    y_halo = [
        remote(charges.at[:, by - R:by], fe.at[own_x, lo_y], 2, yp),
        remote(charges.at[:, 0:R], fe.at[own_x, hi_y], 3, ym),
    ]
    corner = [
        remote(fe.at[bx:bx + R, lo_y], fe.at[lo_x, lo_y], 4, xp),
        remote(fe.at[bx:bx + R, hi_y], fe.at[lo_x, hi_y], 5, xp),
        remote(fe.at[R:2 * R, lo_y], fe.at[hi_x, lo_y], 6, xm),
        remote(fe.at[R:2 * R, hi_y], fe.at[hi_x, hi_y], 7, xm),
    ]
    mown, mlo, mhi = slice(R, R + mx), slice(0, R), slice(R + mx, 2 * R + mx)
    mid_x = [
        remote(me_.at[0, mx:R + mx], me_.at[0, mlo], 8, xp),
        remote(me_.at[0, R:2 * R], me_.at[0, mhi], 9, xm),
    ]
    mid_y = [remote(me_.at[0, mown], me_.at[1, mown], 10, yp)]
    mid_c = [
        remote(me_.at[0, mlo], me_.at[1, mlo], 12, yp),
        remote(me_.at[0, mhi], me_.at[1, mhi], 13, yp),
    ]
    high = 1
    if ngy > 2:
        high = 2
        mid_y.append(remote(me_.at[0, mown], me_.at[2, mown], 11, ym))
        mid_c.append(remote(me_.at[0, mlo], me_.at[2, mlo], 14, ym))
        mid_c.append(remote(me_.at[0, mhi], me_.at[2, mhi], 15, ym))
    z_edge = [
        remote(ze.at[0:R], zr.at[0:R], 16, zm),
        remote(ze.at[R:2 * R], zr.at[R:2 * R], 17, zp),
    ]

    gather = [[], [], []]
    if fused:
        slot = 0
        for axis, part in ((2, ga.at[iy, ix, iz]), (0, ga.at[iy, ix]), (1, ga.at[iy])):
            for off in range(1, sizes[axis]):
                gather[axis].append(pltpu.make_async_remote_copy(
                    src_ref=part, dst_ref=part, send_sem=gs.at[slot], recv_sem=gr.at[slot],
                    device_id=step(axis, off), device_id_type=MESH,
                ))
                slot += 1

    weights_edge = []
    for level in range(2):
        edges = []
        for k in range(TERMS):
            sigma = jnp.full((1, 128), width[level, k], F32)
            rate = 1.0 / (2.0 * sigma * sigma)
            values = [jnp.exp(-(float(t * t) * rate)) for t in range(R + 1)]
            total = values[0]
            for t in range(1, R + 1):
                total = total + 2.0 * values[t]
            inverse = 1.0 / total
            for t in range(R + 1):
                taps[level * TERMS + k, t] = jnp.broadcast_to(values[t] * inverse, (8, 128))
            scale = inverse * weight[level, k]

            def band(d, keep):
                d = d.astype(F32)
                inside = jnp.abs(d) <= float(R)
                if keep is not None:
                    inside = jnp.logical_and(inside, keep)
                return jnp.where(inside, jnp.exp(-(d * d * rate)) * scale, 0.0)

            if level == 0:
                shape = (bz, bz)
                hi, lo = split(band(iota(shape, 0) - iota(shape, 1), None))
                t_hi[0, k * bz:(k + 1) * bz] = hi
                t_lo[0, k * bz:(k + 1) * bz] = lo
                shape = (2 * R, bz)
                row, z = iota(shape, 0), iota(shape, 1)
                edges.append(band(z - jnp.where(row < R, row - R, row - R + bz), None))
            else:
                shape = (bz, bz)
                row = iota(shape, 0)
                for half in range(2):
                    keep = jnp.right_shift(row, mz.bit_length() - 1) == half
                    hi, lo = split(band((row - half * mz) - jnp.right_shift(iota(shape, 1), 1), keep))
                    t_hi[1 + half, k * bz:(k + 1) * bz] = hi
                    t_lo[1 + half, k * bz:(k + 1) * bz] = lo
                shape = (2 * R, bz)
                row, z = iota(shape, 0), iota(shape, 1)
                target = jnp.where(row < R, row - R, row - R + mz)
                pair = [
                    band(z - half * mz - target, jnp.right_shift(z, mz.bit_length() - 1) == half)
                    for half in range(2)
                ]
                edges.append(jnp.concatenate(pair, axis=0))
        weights_edge.append(split(jnp.concatenate(edges, axis=1)))

    local[0].wait()
    halves = []
    for half in range(2):
        rows = []
        for i in range(mx):
            total = None
            for a in range(2):
                for b in range(2):
                    part = fe[R + 2 * i + a, pl.ds(R + half * my + b, R, stride=2), :]
                    total = part if total is None else total + part
            rows.append(total)
        halves.append(jnp.concatenate(rows, axis=0))
    row, col = iota((2 * bz, bz), 0), iota((2 * bz, bz), 1)
    pool = jnp.where(jnp.right_shift(row, 1) == col, 0.125, 0.0).astype(BF16)
    middle = dot2(split(jnp.concatenate(halves, axis=1)), pool)
    me_[0, mown] = middle.reshape(mx, R, bz)
    if fused:
        lanes = []
        for i in range(cx):
            total = None
            for a in range(4):
                for b in range(4):
                    part = fe[R + 4 * i + a, pl.ds(R + b, cy, stride=4), :]
                    total = part if total is None else total + part
            lanes.append(total)
        row, col = iota((cx * bz, bz), 0), iota((cx * bz, bz), 1)
        pool = jnp.where(jnp.right_shift(row, 2) == col, 1.0 / 64.0, 0.0).astype(BF16)
        ga[iy, ix, iz] = dot2(split(jnp.concatenate(lanes, axis=1)), pool)
    pl.semaphore_wait(barrier, greetings)
    for copy in y_halo + x_halo + gather[2] + mid_x + mid_y:
        copy.start()

    for copy in y_halo:
        copy.wait_recv()
    for copy in corner:
        copy.start()
    for copy in gather[2]:
        copy.wait_recv()
    for copy in gather[0]:
        copy.start()

    def taps_of(level, k):
        return [taps[level * TERMS + k, t] for t in range(R + 1)]

    for copy in x_halo:
        copy.wait_recv()

    def x_filter(load, store, level, tiles, length):
        @pl.loop(0, length)
        def _(i):
            g = [taps_of(level, k) for k in range(TERMS)]
            for tile in tiles:
                centre = load(i + R, tile)
                totals = [g[k][0] * centre for k in range(TERMS)]
                for t in range(1, R + 1):
                    pair = load(i + R - t, tile) + load(i + R + t, tile)
                    totals = [totals[k] + g[k][t] * pair for k in range(TERMS)]
                for k in range(TERMS):
                    store(k, i, tile, totals[k])

    def load_f(i, tile):
        return fe[i, tile * 8:tile * 8 + 8, :]

    def store_f(k, i, tile, value):
        x1[k, i, tile * 8:tile * 8 + 8, :] = value

    last = (by + R) // 8
    x_filter(load_f, store_f, 0, range(1, last), bx)

    for copy in mid_x:
        copy.wait_recv()
    for copy in mid_c:
        copy.start()
    for copy in gather[0]:
        copy.wait_recv()
    for copy in gather[1]:
        copy.start()
    for copy in corner:
        copy.wait_recv()
    x_filter(load_f, store_f, 0, (0, last), bx)

    @pl.loop(0, bx)
    def _(i):
        for k in range(TERMS):
            g = taps_of(0, k)
            for pair in range(by // 16):
                base = R + pair * 16
                parts = []
                for s in range(2):
                    at = base + 8 * s
                    total = g[0] * x1[k, i, at:at + 8, :]
                    for t in range(1, R + 1):
                        total = total + g[t] * (
                            x1[k, i, at - t:at - t + 8, :] + x1[k, i, at + t:at + t + 8, :]
                        )
                    parts.append(total)
                hi, lo = split(jnp.concatenate(parts, axis=0))
                rows = pl.ds(pl.multiple_of(i * by + pair * 16, 16), 16)
                ph[rows, k * bz:(k + 1) * bz] = hi
                pl_[rows, k * bz:(k + 1) * bz] = lo

    for copy in mid_y + mid_c:
        copy.wait_recv()
    slots = range(high + 1)

    def load_m(i, slot):
        return me_[slot, i]

    def store_m(k, i, slot, value):
        m1[slot, k, i] = value

    x_filter(load_m, store_m, 1, slots, mx)
    low_lanes = iota((R, bz), 1) < mz

    @pl.loop(0, mx // 2)
    def _(i):
        for k in range(TERMS):
            g = taps_of(1, k)
            parts = []
            for s in range(2):
                own, low, top_ = m1[0, k, 2 * i + s], m1[1, k, 2 * i + s], m1[high, k, 2 * i + s]
                bet[s, 0:8] = pltpu.roll(jnp.where(low_lanes, own, low), mz, 1)
                bet[s, 8:16] = own
                bet[s, 16:24] = pltpu.roll(jnp.where(low_lanes, top_, own), mz, 1)
                total = g[0] * own
                for t in range(1, R + 1):
                    total = total + g[t] * (bet[s, 8 - t:16 - t, :] + bet[s, 8 + t:16 + t, :])
                parts.append(total)
            hi, lo = split(jnp.concatenate(parts, axis=0))
            rows = pl.ds(pl.multiple_of(i * 16, 16), 16)
            mh[rows, k * bz:(k + 1) * bz] = hi
            ml[rows, k * bz:(k + 1) * bz] = lo

    fine = (ph[...], pl_[...])
    mid = (mh[...], ml[...])
    ze[:, 0:bx * by] = dot3(weights_edge[0], fine, NT)
    edge = dot3(weights_edge[1], mid, NT)
    ze[:, bx * by:] = jnp.concatenate([edge[0:2 * R], edge[2 * R:4 * R]], axis=1)
    for copy in z_edge:
        copy.start()

    near = dot3(fine, (t_hi[0], t_lo[0]))
    out[...] = near.reshape(bx, by, bz)
    between = [dot3(mid, (t_hi[1 + half], t_lo[1 + half])) for half in range(2)]

    if fused:
        for copy in local[1:]:
            copy.wait()

        for copy in gather[1]:
            copy.wait_recv()

        group = jnp.right_shift(iota((ngx * ngy * cy, bz), 1), cz.bit_length() - 1)
        blocks = [ga[:, :, j].reshape(ngx * ngy * cy, bz) for j in range(ngz)]
        lines = []
        for i in range(cx):
            line = None
            for j in range(ngz):
                shift = (j * cz - i * cz) % bz
                moved = pltpu.roll(blocks[j], shift, 1) if shift else blocks[j]
                line = moved if line is None else jnp.where(group == j, moved, line)
            lines.append(line)
        lines = jnp.concatenate(lines, axis=0)
        modes = dot3(split(lines), split(qz_v[...]))
        modes = dot3(split(fwd_v[...]), split(modes)) * mult_v[...]
        modes = dot3(split(inv_v[...]), split(modes))
        distant = dot3(split(modes), split(spr_v[...]))
        for i in range(cx):
            part = distant[i * cy:(i + 1) * cy]
            dis[i, pl.ds(0, cy, stride=2), :] = part
            dis[i, pl.ds(1, cy, stride=2), :] = part

    for copy in z_edge:
        copy.wait_recv()
    row, col = iota((2 * R, bz), 0), iota((2 * R, bz), 1)
    place = jnp.where(row < R, row + bz - R, row - R) == col
    place = jnp.where(place, 1.0, 0.0).astype(BF16)
    spread = jnp.where(row < R, row + mz - R, row - R) == jnp.right_shift(col, 1)
    spread = jnp.where(spread, 1.0, 0.0).astype(BF16)
    edge = dot2(split(zr[:, bx * by:].T), spread)
    for half in range(2):
        for i in range(mx):
            at = i * R
            value = between[half][at:at + R] + edge[half * mx * R + at:half * mx * R + at + R]
            if fused:
                value = value + dis[i // 2, half * R:half * R + R, :]
            up[i, pl.ds(2 * R * half, R, stride=2), :] = value
            up[i, pl.ds(2 * R * half + 1, R, stride=2), :] = value
    edge = dot2(split(zr[:, 0:bx * by].T), place)
    for i in range(bx):
        out[i] = out[i] + (edge[i * by:(i + 1) * by] + up[i // 2])

    for copy in x_halo + y_halo + corner + mid_x + mid_y + mid_c + z_edge + sum(gather, []):
        copy.wait_send()


def expand(field):
    return jnp.repeat(jnp.repeat(jnp.repeat(field, 2, axis=0), 2, axis=1), 2, axis=2)


def coarse_of(field):
    s = field.shape
    return field.reshape(s[0] // 4, 4, s[1] // 4, 4, s[2] // 4, 4).mean(axis=(1, 3, 5))


def turn(real, imag, cosine, sine, form, sign):
    ein = functools.partial(jnp.einsum, form, precision=HIGHEST)
    return (
        ein(cosine, real) + sign * ein(sine, imag),
        ein(cosine, imag) - sign * ein(sine, real),
    )


def dft(count):
    modes = np.arange(count)
    angle = 2.0 * np.pi * (modes[:, None] * modes[None, :] % count) / count
    return jnp.asarray(np.cos(angle), F32), jnp.asarray(np.sin(angle), F32)


def solve_top(coarse, sizes):
    bx, by, bz = coarse.shape
    nx, ny, nz = bx * sizes[0], by * sizes[1], bz * sizes[2]
    a2a = functools.partial(lax.all_to_all, tiled=True)
    column = lax.all_gather(coarse, "gx", axis=0, tiled=True)
    tx, ty, tz = dft(nx), dft(ny), dft(nz)
    real, imag = turn(column, jnp.zeros_like(column), *tx, "mx,xyz->myz", 1.0)
    pencil = a2a(jnp.stack([real, imag]), "gy", split_axis=1, concat_axis=2)
    pencil = a2a(pencil, "gz", split_axis=1, concat_axis=3)
    real, imag = turn(pencil[0], pencil[1], *ty, "my,xyz->xmz", 1.0)
    real, imag = turn(real, imag, *tz, "mz,xyz->xym", 1.0)
    rows_y = nx // sizes[1]
    rows = rows_y // sizes[2]
    start = lax.axis_index("gy") * rows_y + lax.axis_index("gz") * rows
    lam_x = jnp.asarray(lam_of(np.arange(nx), nx), F32)
    lam = (
        lax.dynamic_slice_in_dim(lam_x, start, rows, 0)[:, None, None]
        + jnp.asarray(lam_of(np.arange(ny), ny), F32)[None, :, None]
        + jnp.asarray(lam_of(np.arange(nz), nz), F32)[None, None, :]
    )
    mult = jnp.where(lam <= 0.0, 0.0, strength * jnp.exp(-lam) / (lam + screening))
    real, imag = turn(real * mult, imag * mult, *tz, "mz,xyz->xym", -1.0)
    back = a2a(jnp.stack([real, imag]), "gz", split_axis=3, concat_axis=1)
    real, imag = turn(back[0], back[1], *ty, "my,xyz->xmz", -1.0)
    back = a2a(jnp.stack([real, imag]), "gy", split_axis=2, concat_axis=1)
    whole, _ = turn(back[0], back[1], *tx, "mx,xyz->myz", -1.0)
    whole = whole / float(nx * ny * nz)
    return lax.dynamic_slice_in_dim(whole, lax.axis_index("gx") * bx, bx, 0)


def shards(sizes, charges, width, weight):
    bx, by, bz = block = charges.shape
    mx, my = bx // 2, by // 2
    cx, cy, cz = coarse = (bx // 4, by // 4, bz // 4)
    ngx, ngy, ngz = sizes
    count = ngx * ngy * ngz
    points = ngx * cx * ngy * cy
    fused = points <= 512 and ngz * cz == bz and count <= 64
    vmem = pltpu.VMEM
    slots = 2 if ngy == 2 else 3
    scratch = [
        vmem((bx + 2 * R, by + 2 * R, bz), F32),
        vmem((TERMS, bx, by + 2 * R, bz), F32),
        vmem((bx * by, TERMS * bz), BF16),
        vmem((bx * by, TERMS * bz), BF16),
        vmem((slots, mx + 2 * R, R, bz), F32),
        vmem((slots, TERMS, mx, R, bz), F32),
        vmem((mx * R, TERMS * bz), BF16),
        vmem((mx * R, TERMS * bz), BF16),
        vmem((2 * R, bx * by + 2 * mx * R), F32),
        vmem((2 * R, bx * by + 2 * mx * R), F32),
        vmem((3, TERMS * bz, bz), BF16),
        vmem((3, TERMS * bz, bz), BF16),
        vmem((2 * TERMS, R + 1, 8, 128), F32),
        vmem((2, 3 * R, bz), F32),
        vmem((mx, by, bz), F32),
        vmem((cx, my, bz), F32),
        pltpu.SemaphoreType.DMA((18,)),
        pltpu.SemaphoreType.DMA((18,)),
        pltpu.SemaphoreType.DMA((6,)),
    ]
    operands = [charges, width, weight]
    anywhere = pl.BlockSpec(memory_space=pl.ANY)
    small = pl.BlockSpec(memory_space=pltpu.SMEM)
    specs = [anywhere, small, small]
    if fused:
        tables = top_tables(sizes, coarse)
        operands += [jnp.asarray(t) for t in tables]
        specs += [anywhere] * len(tables)
        scratch += [
            vmem((ngy, ngx, ngz, cy, cx * cz), F32),
            vmem(tables[0].shape, F32),
            vmem(tables[1].shape, F32),
            vmem(tables[2].shape, F32),
            vmem(tables[3].shape[1:], F32),
            vmem(tables[4].shape[1:], F32),
            pltpu.SemaphoreType.DMA((ngx + ngy + ngz - 3,)),
            pltpu.SemaphoreType.DMA((ngx + ngy + ngz - 3,)),
        ]
    result = pl.pallas_call(
        functools.partial(body, sizes, block, fused),
        out_shape=jax.ShapeDtypeStruct(block, F32),
        in_specs=specs,
        out_specs=pl.BlockSpec(memory_space=pltpu.VMEM),
        scratch_shapes=scratch,
        compiler_params=pltpu.CompilerParams(collective_id=0, has_side_effects=True),
    )(*operands)
    if not fused:
        result = result + expand(expand(solve_top(coarse_of(charges), sizes)))
    return result


def solution(mesh):
    sizes = tuple(mesh.shape[a] for a in AXES)
    placed = (P(*AXES), P(), P())
    return jax.shard_map(
        functools.partial(shards, sizes), mesh=mesh, in_specs=placed, out_specs=P(*AXES),
        check_vma=False,
    )
```

```python
import functools
import math

import jax
import jax.numpy as jnp
import numpy as np
from jax import lax
from jax.experimental import pallas as pl
from jax.experimental.pallas import tpu as pltpu
from jax.sharding import PartitionSpec as P

TERMS = 4
R = 8
HIGHEST = lax.Precision.HIGHEST
screening = 0.01
strength = 4.0
AXES = ("gx", "gy", "gz")
MESH = pl.DeviceIdType.MESH
F32 = jnp.float32
BF16 = jnp.bfloat16


def real_basis(count):
    points = np.arange(count)
    rows, freqs = [], []
    for m in range(count // 2 + 1):
        angle = 2.0 * np.pi * ((m * points) % count) / count
        single = m == 0 or 2 * m == count
        scale = math.sqrt((1.0 if single else 2.0) / count)
        rows.append(scale * np.cos(angle))
        freqs.append(m)
        if not single:
            rows.append(scale * np.sin(angle))
            freqs.append(m)
    return np.stack(rows), np.array(freqs)


def lam_of(freqs, count):
    return 2.0 - 2.0 * np.cos(2.0 * np.pi * freqs / count)


def top_tables(sizes, block):
    ngx, ngy, ngz = sizes
    cx, cy, cz = block
    nx, ny, nz = ngx * cx, ngy * cy, ngz * cz
    (qx, fx), (qy, fy), (qz, fz) = real_basis(nx), real_basis(ny), real_basis(nz)
    lam = (
        lam_of(fx, nx)[:, None, None] + lam_of(fy, ny)[None, :, None] + lam_of(fz, nz)[None, None, :]
    )
    zero = (fx[:, None, None] + fy[None, :, None] + fz[None, None, :]) == 0
    mult = np.where(zero, 0.0, strength * np.exp(-lam) / (lam + screening)).reshape(nx * ny, nz)
    kron = np.kron(qx, qy).reshape(nx * ny, ngx, cx, ngy, cy)
    forward = kron.transpose(0, 2, 3, 1, 4).reshape(nx * ny, nx * ny)
    inverse = kron.transpose(1, 3, 2, 4, 0).reshape(ngx * ngy, cx * cy, nx * ny)
    spread = np.repeat(qz, 4, axis=1).reshape(nz, ngz, 4 * cz).transpose(1, 0, 2)
    return [np.asarray(t, np.float32) for t in (qz.T, forward, mult, inverse, spread)]


def split(value):
    high = value.astype(BF16)
    return high, (value - high.astype(F32)).astype(BF16)


NN = (((1,), (0,)), ((), ()))
NT = (((1,), (1,)), ((), ()))


def mm(a, b, dims=NN):
    return lax.dot_general(a, b, dims, preferred_element_type=F32)


def dot3(a, b, dims=NN):
    (ah, al), (bh, bl) = a, b
    return mm(ah, bh, dims) + (mm(al, bh, dims) + mm(ah, bl, dims))


def dot2(a, exact):
    return mm(a[0], exact) + mm(a[1], exact)


def iota(shape, dim):
    return lax.broadcasted_iota(jnp.int32, shape, dim)


def body(sizes, block, fused, *refs):
    ngx, ngy, ngz = sizes
    bx, by, bz = block
    mx, my, mz = bx // 2, by // 2, bz // 2
    cx, cy, cz = bx // 4, by // 4, bz // 4
    if fused:
        (charges, width, weight, qz_h, fwd_h, mult_h, inv_h, spr_h, out) = refs[:9]
        refs = refs[9:]
    else:
        (charges, width, weight, out) = refs[:4]
        refs = refs[4:]
    (fe, x1, ph, pl_, me_, m1, mh, ml, ze, zr, zem, zrm, t_hi, t_lo, taps, bet, up, dis, ssem, rsem, lsem) = refs[:21]
    if fused:
        (ga, qz_v, fwd_v, mult_v, inv_v, spr_v, gs, gr) = refs[21:]

    ix, iy, iz = (lax.axis_index(a) for a in AXES)

    def step(axis, by_):
        position = [ix, iy, iz]
        n = sizes[axis]
        position[axis] = lax.rem(position[axis] + by_ + n, n)
        return tuple(position)

    barrier = pltpu.get_barrier_semaphore()
    greetings = 0
    for axis in range(3):
        n = sizes[axis]
        for off in range(1, n) if fused else ((1, -1) if n > 2 else (1,)):
            pl.semaphore_signal(barrier, 1, device_id=step(axis, off), device_id_type=MESH)
            greetings += 1

    local = [pltpu.make_async_copy(charges, fe.at[R:R + bx, R:R + by], lsem.at[0])]
    if fused:
        local += [
            pltpu.make_async_copy(qz_h, qz_v, lsem.at[1]),
            pltpu.make_async_copy(fwd_h, fwd_v, lsem.at[2]),
            pltpu.make_async_copy(mult_h, mult_v, lsem.at[3]),
            pltpu.make_async_copy(inv_h.at[ix * ngy + iy], inv_v, lsem.at[4]),
            pltpu.make_async_copy(spr_h.at[iz], spr_v, lsem.at[5]),
        ]
    for copy in local:
        copy.start()

    def remote(src, dst, slot, target):
        return pltpu.make_async_remote_copy(
            src_ref=src, dst_ref=dst, send_sem=ssem.at[slot], recv_sem=rsem.at[slot],
            device_id=target, device_id_type=MESH,
        )

    xp, xm, yp, ym, zp, zm = step(0, 1), step(0, -1), step(1, 1), step(1, -1), step(2, 1), step(2, -1)
    lo_x, hi_x, lo_y, hi_y = slice(0, R), slice(R + bx, 2 * R + bx), slice(0, R), slice(R + by, 2 * R + by)
    own_x, own_y = slice(R, R + bx), slice(R, R + by)
    x_halo = [
        remote(charges.at[bx - R:bx], fe.at[lo_x, own_y], 0, xp),
        remote(charges.at[0:R], fe.at[hi_x, own_y], 1, xm),
    ]
    y_halo = [
        remote(charges.at[:, by - R:by], fe.at[own_x, lo_y], 2, yp),
        remote(charges.at[:, 0:R], fe.at[own_x, hi_y], 3, ym),
    ]
    corner = [
        remote(fe.at[bx:bx + R, lo_y], fe.at[lo_x, lo_y], 4, xp),
        remote(fe.at[bx:bx + R, hi_y], fe.at[lo_x, hi_y], 5, xp),
        remote(fe.at[R:2 * R, lo_y], fe.at[hi_x, lo_y], 6, xm),
        remote(fe.at[R:2 * R, hi_y], fe.at[hi_x, hi_y], 7, xm),
    ]
    mown, mlo, mhi = slice(R, R + mx), slice(0, R), slice(R + mx, 2 * R + mx)
    mid_x = [
        remote(me_.at[0, mx:R + mx], me_.at[0, mlo], 8, xp),
        remote(me_.at[0, R:2 * R], me_.at[0, mhi], 9, xm),
    ]
    mid_y = [remote(me_.at[0, mown], me_.at[1, mown], 10, yp)]
    mid_c = [
        remote(me_.at[0, mlo], me_.at[1, mlo], 12, yp),
        remote(me_.at[0, mhi], me_.at[1, mhi], 13, yp),
    ]
    high = 1
    if ngy > 2:
        high = 2
        mid_y.append(remote(me_.at[0, mown], me_.at[2, mown], 11, ym))
        mid_c.append(remote(me_.at[0, mlo], me_.at[2, mlo], 14, ym))
        mid_c.append(remote(me_.at[0, mhi], me_.at[2, mhi], 15, ym))
    z_edge = [
        remote(ze.at[0:R], zr.at[0:R], 16, zm),
        remote(ze.at[R:2 * R], zr.at[R:2 * R], 17, zp),
    ]
    z_mid = [
        remote(zem.at[0:R], zrm.at[0:R], 18, zm),
        remote(zem.at[R:2 * R], zrm.at[R:2 * R], 19, zp),
    ]

    gather = [[], [], []]
    if fused:
        slot = 0
        for axis, part in ((2, ga.at[iy, ix, iz]), (0, ga.at[iy, ix]), (1, ga.at[iy])):
            for off in range(1, sizes[axis]):
                gather[axis].append(pltpu.make_async_remote_copy(
                    src_ref=part, dst_ref=part, send_sem=gs.at[slot], recv_sem=gr.at[slot],
                    device_id=step(axis, off), device_id_type=MESH,
                ))
                slot += 1

    weights_edge = []
    for level in range(2):
        edges = []
        for k in range(TERMS):
            sigma = jnp.full((1, 128), width[level, k], F32)
            rate = 1.0 / (2.0 * sigma * sigma)
            values = [jnp.exp(-(float(t * t) * rate)) for t in range(R + 1)]
            total = values[0]
            for t in range(1, R + 1):
                total = total + 2.0 * values[t]
            inverse = 1.0 / total
            for t in range(R + 1):
                taps[level * TERMS + k, t] = jnp.broadcast_to(values[t] * inverse, (8, 128))
            scale = inverse * weight[level, k]

            def band(d, keep):
                d = d.astype(F32)
                inside = jnp.abs(d) <= float(R)
                if keep is not None:
                    inside = jnp.logical_and(inside, keep)
                return jnp.where(inside, jnp.exp(-(d * d * rate)) * scale, 0.0)

            if level == 0:
                shape = (bz, bz)
                hi, lo = split(band(iota(shape, 0) - iota(shape, 1), None))
                t_hi[0, k * bz:(k + 1) * bz] = hi
                t_lo[0, k * bz:(k + 1) * bz] = lo
                shape = (2 * R, bz)
                row, z = iota(shape, 0), iota(shape, 1)
                edges.append(band(z - jnp.where(row < R, row - R, row - R + bz), None))
            else:
                shape = (bz, bz)
                row = iota(shape, 0)
                for half in range(2):
                    keep = jnp.right_shift(row, mz.bit_length() - 1) == half
                    hi, lo = split(band((row - half * mz) - jnp.right_shift(iota(shape, 1), 1), keep))
                    t_hi[1 + half, k * bz:(k + 1) * bz] = hi
                    t_lo[1 + half, k * bz:(k + 1) * bz] = lo
                shape = (2 * R, bz)
                row, z = iota(shape, 0), iota(shape, 1)
                target = jnp.where(row < R, row - R, row - R + mz)
                pair = [
                    band(z - half * mz - target, jnp.right_shift(z, mz.bit_length() - 1) == half)
                    for half in range(2)
                ]
                edges.append(jnp.concatenate(pair, axis=0))
        weights_edge.append(split(jnp.concatenate(edges, axis=1)))

    local[0].wait()
    halves = []
    for half in range(2):
        rows = []
        for i in range(mx):
            total = None
            for a in range(2):
                for b in range(2):
                    part = fe[R + 2 * i + a, pl.ds(R + half * my + b, R, stride=2), :]
                    total = part if total is None else total + part
            rows.append(total)
        halves.append(jnp.concatenate(rows, axis=0))
    row, col = iota((2 * bz, bz), 0), iota((2 * bz, bz), 1)
    pool = jnp.where(jnp.right_shift(row, 1) == col, 0.125, 0.0).astype(BF16)
    middle = dot2(split(jnp.concatenate(halves, axis=1)), pool)
    me_[0, mown] = middle.reshape(mx, R, bz)
    if fused:
        lanes = []
        for i in range(cx):
            total = None
            for a in range(4):
                for b in range(4):
                    part = fe[R + 4 * i + a, pl.ds(R + b, cy, stride=4), :]
                    total = part if total is None else total + part
            lanes.append(total)
        row, col = iota((cx * bz, bz), 0), iota((cx * bz, bz), 1)
        pool = jnp.where(jnp.right_shift(row, 2) == col, 1.0 / 64.0, 0.0).astype(BF16)
        ga[iy, ix, iz] = dot2(split(jnp.concatenate(lanes, axis=1)), pool)
    pl.semaphore_wait(barrier, greetings)
    for copy in mid_x + mid_y + gather[2] + y_halo + x_halo:
        copy.start()

    for copy in mid_x:
        copy.wait_recv()
    for copy in mid_c:
        copy.start()
    for copy in y_halo:
        copy.wait_recv()
    for copy in corner:
        copy.start()
    for copy in gather[2]:
        copy.wait_recv()
    for copy in gather[0]:
        copy.start()

    def taps_of(level, k):
        return [taps[level * TERMS + k, t] for t in range(R + 1)]

    for copy in x_halo:
        copy.wait_recv()

    def x_filter(load, store, level, tiles, length):
        @pl.loop(0, length)
        def _(i):
            g = [taps_of(level, k) for k in range(TERMS)]
            for tile in tiles:
                centre = load(i + R, tile)
                totals = [g[k][0] * centre for k in range(TERMS)]
                for t in range(1, R + 1):
                    pair = load(i + R - t, tile) + load(i + R + t, tile)
                    totals = [totals[k] + g[k][t] * pair for k in range(TERMS)]
                for k in range(TERMS):
                    store(k, i, tile, totals[k])

    def load_f(i, tile):
        return fe[i, tile * 8:tile * 8 + 8, :]

    def store_f(k, i, tile, value):
        x1[k, i, tile * 8:tile * 8 + 8, :] = value

    last = (by + R) // 8
    x_filter(load_f, store_f, 0, range(1, last), bx)

    for copy in mid_y + mid_c:
        copy.wait_recv()
    slots = range(high + 1)

    def load_m(i, slot):
        return me_[slot, i]

    def store_m(k, i, slot, value):
        m1[slot, k, i] = value

    x_filter(load_m, store_m, 1, slots, mx)
    low_lanes = iota((R, bz), 1) < mz

    @pl.loop(0, mx // 2)
    def _(i):
        for k in range(TERMS):
            g = taps_of(1, k)
            parts = []
            for s in range(2):
                own, low, top_ = m1[0, k, 2 * i + s], m1[1, k, 2 * i + s], m1[high, k, 2 * i + s]
                bet[s, 0:8] = pltpu.roll(jnp.where(low_lanes, own, low), mz, 1)
                bet[s, 8:16] = own
                bet[s, 16:24] = pltpu.roll(jnp.where(low_lanes, top_, own), mz, 1)
                total = g[0] * own
                for t in range(1, R + 1):
                    total = total + g[t] * (bet[s, 8 - t:16 - t, :] + bet[s, 8 + t:16 + t, :])
                parts.append(total)
            hi, lo = split(jnp.concatenate(parts, axis=0))
            rows = pl.ds(pl.multiple_of(i * 16, 16), 16)
            mh[rows, k * bz:(k + 1) * bz] = hi
            ml[rows, k * bz:(k + 1) * bz] = lo

    mid = (mh[...], ml[...])
    edge = dot3(weights_edge[1], mid, NT)
    zem[...] = jnp.concatenate([edge[0:2 * R], edge[2 * R:4 * R]], axis=1)
    for copy in z_mid:
        copy.start()
    between = [dot3(mid, (t_hi[1 + half], t_lo[1 + half])) for half in range(2)]
    for copy in gather[0]:
        copy.wait_recv()
    for copy in gather[1]:
        copy.start()

    for copy in corner:
        copy.wait_recv()
    x_filter(load_f, store_f, 0, (0, last), bx)

    @pl.loop(0, bx)
    def _(i):
        for k in range(TERMS):
            g = taps_of(0, k)
            for pair in range(by // 16):
                base = R + pair * 16
                parts = []
                for s in range(2):
                    at = base + 8 * s
                    total = g[0] * x1[k, i, at:at + 8, :]
                    for t in range(1, R + 1):
                        total = total + g[t] * (
                            x1[k, i, at - t:at - t + 8, :] + x1[k, i, at + t:at + t + 8, :]
                        )
                    parts.append(total)
                hi, lo = split(jnp.concatenate(parts, axis=0))
                rows = pl.ds(pl.multiple_of(i * by + pair * 16, 16), 16)
                ph[rows, k * bz:(k + 1) * bz] = hi
                pl_[rows, k * bz:(k + 1) * bz] = lo

    fine = (ph[...], pl_[...])
    ze[...] = dot3(weights_edge[0], fine, NT)
    for copy in z_edge:
        copy.start()
    near = dot3(fine, (t_hi[0], t_lo[0]))
    out[...] = near.reshape(bx, by, bz)

    if fused:
        for copy in local[1:]:
            copy.wait()

        for copy in gather[1]:
            copy.wait_recv()

        group = jnp.right_shift(iota((ngx * ngy * cy, bz), 1), cz.bit_length() - 1)
        blocks = [ga[:, :, j].reshape(ngx * ngy * cy, bz) for j in range(ngz)]
        lines = []
        for i in range(cx):
            line = None
            for j in range(ngz):
                shift = (j * cz - i * cz) % bz
                moved = pltpu.roll(blocks[j], shift, 1) if shift else blocks[j]
                line = moved if line is None else jnp.where(group == j, moved, line)
            lines.append(line)
        lines = jnp.concatenate(lines, axis=0)
        modes = dot3(split(lines), split(qz_v[...]))
        modes = dot3(split(fwd_v[...]), split(modes)) * mult_v[...]
        modes = dot3(split(inv_v[...]), split(modes))
        distant = dot3(split(modes), split(spr_v[...]))
        for i in range(cx):
            part = distant[i * cy:(i + 1) * cy]
            dis[i, pl.ds(0, cy, stride=2), :] = part
            dis[i, pl.ds(1, cy, stride=2), :] = part

    for copy in z_mid:
        copy.wait_recv()
    row, col = iota((2 * R, bz), 0), iota((2 * R, bz), 1)
    place = jnp.where(row < R, row + bz - R, row - R) == col
    place = jnp.where(place, 1.0, 0.0).astype(BF16)
    spread = jnp.where(row < R, row + mz - R, row - R) == jnp.right_shift(col, 1)
    spread = jnp.where(spread, 1.0, 0.0).astype(BF16)
    edge = dot2(split(zrm[...].T), spread)
    for half in range(2):
        for i in range(mx):
            at = i * R
            value = between[half][at:at + R] + edge[half * mx * R + at:half * mx * R + at + R]
            if fused:
                value = value + dis[i // 2, half * R:half * R + R, :]
            up[i, pl.ds(2 * R * half, R, stride=2), :] = value
            up[i, pl.ds(2 * R * half + 1, R, stride=2), :] = value
    for copy in z_edge:
        copy.wait_recv()
    edge = dot2(split(zr[...].T), place)
    for i in range(bx):
        out[i] = out[i] + (edge[i * by:(i + 1) * by] + up[i // 2])

    for copy in x_halo + y_halo + corner + mid_x + mid_y + mid_c + z_mid + z_edge + sum(gather, []):
        copy.wait_send()


def expand(field):
    return jnp.repeat(jnp.repeat(jnp.repeat(field, 2, axis=0), 2, axis=1), 2, axis=2)


def coarse_of(field):
    s = field.shape
    return field.reshape(s[0] // 4, 4, s[1] // 4, 4, s[2] // 4, 4).mean(axis=(1, 3, 5))


def turn(real, imag, cosine, sine, form, sign):
    ein = functools.partial(jnp.einsum, form, precision=HIGHEST)
    return (
        ein(cosine, real) + sign * ein(sine, imag),
        ein(cosine, imag) - sign * ein(sine, real),
    )


def dft(count):
    modes = np.arange(count)
    angle = 2.0 * np.pi * (modes[:, None] * modes[None, :] % count) / count
    return jnp.asarray(np.cos(angle), F32), jnp.asarray(np.sin(angle), F32)


def solve_top(coarse, sizes):
    bx, by, bz = coarse.shape
    nx, ny, nz = bx * sizes[0], by * sizes[1], bz * sizes[2]
    a2a = functools.partial(lax.all_to_all, tiled=True)
    column = lax.all_gather(coarse, "gx", axis=0, tiled=True)
    tx, ty, tz = dft(nx), dft(ny), dft(nz)
    real, imag = turn(column, jnp.zeros_like(column), *tx, "mx,xyz->myz", 1.0)
    pencil = a2a(jnp.stack([real, imag]), "gy", split_axis=1, concat_axis=2)
    pencil = a2a(pencil, "gz", split_axis=1, concat_axis=3)
    real, imag = turn(pencil[0], pencil[1], *ty, "my,xyz->xmz", 1.0)
    real, imag = turn(real, imag, *tz, "mz,xyz->xym", 1.0)
    rows_y = nx // sizes[1]
    rows = rows_y // sizes[2]
    start = lax.axis_index("gy") * rows_y + lax.axis_index("gz") * rows
    lam_x = jnp.asarray(lam_of(np.arange(nx), nx), F32)
    lam = (
        lax.dynamic_slice_in_dim(lam_x, start, rows, 0)[:, None, None]
        + jnp.asarray(lam_of(np.arange(ny), ny), F32)[None, :, None]
        + jnp.asarray(lam_of(np.arange(nz), nz), F32)[None, None, :]
    )
    mult = jnp.where(lam <= 0.0, 0.0, strength * jnp.exp(-lam) / (lam + screening))
    real, imag = turn(real * mult, imag * mult, *tz, "mz,xyz->xym", -1.0)
    back = a2a(jnp.stack([real, imag]), "gz", split_axis=3, concat_axis=1)
    real, imag = turn(back[0], back[1], *ty, "my,xyz->xmz", -1.0)
    back = a2a(jnp.stack([real, imag]), "gy", split_axis=2, concat_axis=1)
    whole, _ = turn(back[0], back[1], *tx, "mx,xyz->myz", -1.0)
    whole = whole / float(nx * ny * nz)
    return lax.dynamic_slice_in_dim(whole, lax.axis_index("gx") * bx, bx, 0)


def shards(sizes, charges, width, weight):
    bx, by, bz = block = charges.shape
    mx, my = bx // 2, by // 2
    cx, cy, cz = coarse = (bx // 4, by // 4, bz // 4)
    ngx, ngy, ngz = sizes
    count = ngx * ngy * ngz
    points = ngx * cx * ngy * cy
    fused = points <= 512 and ngz * cz == bz and count <= 64
    vmem = pltpu.VMEM
    slots = 2 if ngy == 2 else 3
    scratch = [
        vmem((bx + 2 * R, by + 2 * R, bz), F32),
        vmem((TERMS, bx, by + 2 * R, bz), F32),
        vmem((bx * by, TERMS * bz), BF16),
        vmem((bx * by, TERMS * bz), BF16),
        vmem((slots, mx + 2 * R, R, bz), F32),
        vmem((slots, TERMS, mx, R, bz), F32),
        vmem((mx * R, TERMS * bz), BF16),
        vmem((mx * R, TERMS * bz), BF16),
        vmem((2 * R, bx * by), F32),
        vmem((2 * R, bx * by), F32),
        vmem((2 * R, 2 * mx * R), F32),
        vmem((2 * R, 2 * mx * R), F32),
        vmem((3, TERMS * bz, bz), BF16),
        vmem((3, TERMS * bz, bz), BF16),
        vmem((2 * TERMS, R + 1, 8, 128), F32),
        vmem((2, 3 * R, bz), F32),
        vmem((mx, by, bz), F32),
        vmem((cx, my, bz), F32),
        pltpu.SemaphoreType.DMA((20,)),
        pltpu.SemaphoreType.DMA((20,)),
        pltpu.SemaphoreType.DMA((6,)),
    ]
    operands = [charges, width, weight]
    anywhere = pl.BlockSpec(memory_space=pl.ANY)
    small = pl.BlockSpec(memory_space=pltpu.SMEM)
    specs = [anywhere, small, small]
    if fused:
        tables = top_tables(sizes, coarse)
        operands += [jnp.asarray(t) for t in tables]
        specs += [anywhere] * len(tables)
        scratch += [
            vmem((ngy, ngx, ngz, cy, cx * cz), F32),
            vmem(tables[0].shape, F32),
            vmem(tables[1].shape, F32),
            vmem(tables[2].shape, F32),
            vmem(tables[3].shape[1:], F32),
            vmem(tables[4].shape[1:], F32),
            pltpu.SemaphoreType.DMA((ngx + ngy + ngz - 3,)),
            pltpu.SemaphoreType.DMA((ngx + ngy + ngz - 3,)),
        ]
    result = pl.pallas_call(
        functools.partial(body, sizes, block, fused),
        out_shape=pltpu.VMEM(block, F32),
        in_specs=specs,
        out_specs=pl.BlockSpec(memory_space=pltpu.VMEM),
        scratch_shapes=scratch,
        compiler_params=pltpu.CompilerParams(collective_id=0, has_side_effects=True),
    )(*operands)
    if not fused:
        result = result + expand(expand(solve_top(coarse_of(charges), sizes)))
    return result


def solution(mesh):
    sizes = tuple(mesh.shape[a] for a in AXES)
    placed = (P(*AXES), P(), P())
    return jax.shard_map(
        functools.partial(shards, sizes), mesh=mesh, in_specs=placed, out_specs=P(*AXES),
        check_vma=False,
    )
```

```python
import functools
import math

import jax
import jax.numpy as jnp
import numpy as np
from jax import lax
from jax.experimental import pallas as pl
from jax.experimental.pallas import tpu as pltpu
from jax.sharding import PartitionSpec as P

TERMS = 4
R = 8
HIGHEST = lax.Precision.HIGHEST
screening = 0.01
strength = 4.0
AXES = ("gx", "gy", "gz")
MESH = pl.DeviceIdType.MESH
F32 = jnp.float32
BF16 = jnp.bfloat16


def real_basis(count):
    points = np.arange(count)
    rows, freqs = [], []
    for m in range(count // 2 + 1):
        angle = 2.0 * np.pi * ((m * points) % count) / count
        single = m == 0 or 2 * m == count
        scale = math.sqrt((1.0 if single else 2.0) / count)
        rows.append(scale * np.cos(angle))
        freqs.append(m)
        if not single:
            rows.append(scale * np.sin(angle))
            freqs.append(m)
    return np.stack(rows), np.array(freqs)


def lam_of(freqs, count):
    return 2.0 - 2.0 * np.cos(2.0 * np.pi * freqs / count)


def top_tables(sizes, block):
    ngx, ngy, ngz = sizes
    cx, cy, cz = block
    nx, ny, nz = ngx * cx, ngy * cy, ngz * cz
    (qx, fx), (qy, fy), (qz, fz) = real_basis(nx), real_basis(ny), real_basis(nz)
    lam = (
        lam_of(fx, nx)[:, None, None] + lam_of(fy, ny)[None, :, None] + lam_of(fz, nz)[None, None, :]
    )
    zero = (fx[:, None, None] + fy[None, :, None] + fz[None, None, :]) == 0
    mult = np.where(zero, 0.0, strength * np.exp(-lam) / (lam + screening)).reshape(nx * ny, nz)
    kron = np.kron(qx, qy).reshape(nx * ny, ngx, cx, ngy, cy)
    forward = kron.transpose(0, 2, 3, 1, 4).reshape(nx * ny, nx * ny)
    inverse = kron.transpose(1, 3, 2, 4, 0).reshape(ngx * ngy, cx * cy, nx * ny)
    spread = np.repeat(qz, 4, axis=1).reshape(nz, ngz, 4 * cz).transpose(1, 0, 2)
    return [np.asarray(t, np.float32) for t in (qz.T, forward, mult, inverse, spread)]


def split(value):
    high = value.astype(BF16)
    return high, (value - high.astype(F32)).astype(BF16)


NN = (((1,), (0,)), ((), ()))
NT = (((1,), (1,)), ((), ()))


def mm(a, b, dims=NN):
    return lax.dot_general(a, b, dims, preferred_element_type=F32)


def dot3(a, b, dims=NN):
    (ah, al), (bh, bl) = a, b
    return mm(ah, bh, dims) + (mm(al, bh, dims) + mm(ah, bl, dims))


def dot2(a, exact):
    return mm(a[0], exact) + mm(a[1], exact)


def iota(shape, dim):
    return lax.broadcasted_iota(jnp.int32, shape, dim)


def body(sizes, block, fused, *refs):
    ngx, ngy, ngz = sizes
    bx, by, bz = block
    mx, my, mz = bx // 2, by // 2, bz // 2
    cx, cy, cz = bx // 4, by // 4, bz // 4
    if fused:
        (charges, width, weight, qz_h, fwd_h, mult_h, inv_h, spr_h, out) = refs[:9]
        refs = refs[9:]
    else:
        (charges, width, weight, out) = refs[:4]
        refs = refs[4:]
    (fe, x1, ph, pl_, me_, m1, mh, ml, ze, zr, zem, zrm, t_hi, t_lo, taps, bet, up, dis, ssem, rsem, lsem) = refs[:21]
    if fused:
        (ga, qz_v, fwd_v, mult_v, inv_v, spr_v, gs, gr) = refs[21:]

    ix, iy, iz = (lax.axis_index(a) for a in AXES)

    def step(axis, by_):
        position = [ix, iy, iz]
        n = sizes[axis]
        position[axis] = lax.rem(position[axis] + by_ + n, n)
        return tuple(position)

    barrier = pltpu.get_barrier_semaphore()
    greetings = 0
    for axis in range(3):
        n = sizes[axis]
        for off in range(1, n) if fused else ((1, -1) if n > 2 else (1,)):
            pl.semaphore_signal(barrier, 1, device_id=step(axis, off), device_id_type=MESH)
            greetings += 1

    local = [pltpu.make_async_copy(charges, fe.at[R:R + bx, R:R + by], lsem.at[0])]
    if fused:
        local += [
            pltpu.make_async_copy(qz_h, qz_v, lsem.at[1]),
            pltpu.make_async_copy(fwd_h, fwd_v, lsem.at[2]),
            pltpu.make_async_copy(mult_h, mult_v, lsem.at[3]),
            pltpu.make_async_copy(inv_h.at[ix * ngy + iy], inv_v, lsem.at[4]),
            pltpu.make_async_copy(spr_h.at[iz], spr_v, lsem.at[5]),
        ]
    for copy in local:
        copy.start()

    def remote(src, dst, slot, target):
        return pltpu.make_async_remote_copy(
            src_ref=src, dst_ref=dst, send_sem=ssem.at[slot], recv_sem=rsem.at[slot],
            device_id=target, device_id_type=MESH,
        )

    xp, xm, yp, ym, zp, zm = step(0, 1), step(0, -1), step(1, 1), step(1, -1), step(2, 1), step(2, -1)
    lo_x, hi_x, lo_y, hi_y = slice(0, R), slice(R + bx, 2 * R + bx), slice(0, R), slice(R + by, 2 * R + by)
    own_x, own_y = slice(R, R + bx), slice(R, R + by)
    x_halo = [
        remote(charges.at[bx - R:bx], fe.at[lo_x, own_y], 0, xp),
        remote(charges.at[0:R], fe.at[hi_x, own_y], 1, xm),
    ]
    y_halo = [
        remote(charges.at[:, by - R:by], fe.at[own_x, lo_y], 2, yp),
        remote(charges.at[:, 0:R], fe.at[own_x, hi_y], 3, ym),
    ]
    corner = [
        remote(fe.at[bx:bx + R, lo_y], fe.at[lo_x, lo_y], 4, xp),
        remote(fe.at[bx:bx + R, hi_y], fe.at[lo_x, hi_y], 5, xp),
        remote(fe.at[R:2 * R, lo_y], fe.at[hi_x, lo_y], 6, xm),
        remote(fe.at[R:2 * R, hi_y], fe.at[hi_x, hi_y], 7, xm),
    ]
    mown, mlo, mhi = slice(R, R + mx), slice(0, R), slice(R + mx, 2 * R + mx)
    mid_x = [
        remote(me_.at[0, mx:R + mx], me_.at[0, mlo], 8, xp),
        remote(me_.at[0, R:2 * R], me_.at[0, mhi], 9, xm),
    ]
    mid_y = [remote(me_.at[0, mown], me_.at[1, mown], 10, yp)]
    mid_c = [
        remote(me_.at[0, mlo], me_.at[1, mlo], 12, yp),
        remote(me_.at[0, mhi], me_.at[1, mhi], 13, yp),
    ]
    high = 1
    if ngy > 2:
        high = 2
        mid_y.append(remote(me_.at[0, mown], me_.at[2, mown], 11, ym))
        mid_c.append(remote(me_.at[0, mlo], me_.at[2, mlo], 14, ym))
        mid_c.append(remote(me_.at[0, mhi], me_.at[2, mhi], 15, ym))
    z_edge = [
        remote(ze.at[0:R], zr.at[0:R], 16, zm),
        remote(ze.at[R:2 * R], zr.at[R:2 * R], 17, zp),
    ]
    z_mid = [
        remote(zem.at[0:R], zrm.at[0:R], 18, zm),
        remote(zem.at[R:2 * R], zrm.at[R:2 * R], 19, zp),
    ]

    gather = [[], [], []]
    if fused:
        slot = 0
        for axis, part in ((2, ga.at[iy, ix, iz]), (0, ga.at[iy, ix]), (1, ga.at[iy])):
            for off in range(1, sizes[axis]):
                gather[axis].append(pltpu.make_async_remote_copy(
                    src_ref=part, dst_ref=part, send_sem=gs.at[slot], recv_sem=gr.at[slot],
                    device_id=step(axis, off), device_id_type=MESH,
                ))
                slot += 1

    weights_edge = []
    for level in range(2):
        edges = []
        for k in range(TERMS):
            sigma = jnp.full((1, 128), width[level, k], F32)
            rate = 1.0 / (2.0 * sigma * sigma)
            values = [jnp.exp(-(float(t * t) * rate)) for t in range(R + 1)]
            total = values[0]
            for t in range(1, R + 1):
                total = total + 2.0 * values[t]
            inverse = 1.0 / total
            for t in range(R + 1):
                taps[level * TERMS + k, t] = jnp.broadcast_to(values[t] * inverse, (8, 128))
            scale = inverse * weight[level, k]

            def band(d, keep):
                d = d.astype(F32)
                inside = jnp.abs(d) <= float(R)
                if keep is not None:
                    inside = jnp.logical_and(inside, keep)
                return jnp.where(inside, jnp.exp(-(d * d * rate)) * scale, 0.0)

            if level == 0:
                shape = (bz, bz)
                hi, lo = split(band(iota(shape, 0) - iota(shape, 1), None))
                t_hi[0, k * bz:(k + 1) * bz] = hi
                t_lo[0, k * bz:(k + 1) * bz] = lo
                shape = (2 * R, bz)
                row, z = iota(shape, 0), iota(shape, 1)
                edges.append(band(z - jnp.where(row < R, row - R, row - R + bz), None))
            else:
                shape = (bz, bz)
                row = iota(shape, 0)
                for half in range(2):
                    keep = jnp.right_shift(row, mz.bit_length() - 1) == half
                    hi, lo = split(band((row - half * mz) - jnp.right_shift(iota(shape, 1), 1), keep))
                    t_hi[1 + half, k * bz:(k + 1) * bz] = hi
                    t_lo[1 + half, k * bz:(k + 1) * bz] = lo
                shape = (2 * R, bz)
                row, z = iota(shape, 0), iota(shape, 1)
                target = jnp.where(row < R, row - R, row - R + mz)
                pair = [
                    band(z - half * mz - target, jnp.right_shift(z, mz.bit_length() - 1) == half)
                    for half in range(2)
                ]
                edges.append(jnp.concatenate(pair, axis=0))
        weights_edge.append(split(jnp.concatenate(edges, axis=1)))

    local[0].wait()
    halves = []
    for half in range(2):
        rows = []
        for i in range(mx):
            total = None
            for a in range(2):
                for b in range(2):
                    part = fe[R + 2 * i + a, pl.ds(R + half * my + b, R, stride=2), :]
                    total = part if total is None else total + part
            rows.append(total)
        halves.append(jnp.concatenate(rows, axis=0))
    row, col = iota((2 * bz, bz), 0), iota((2 * bz, bz), 1)
    pool = jnp.where(jnp.right_shift(row, 1) == col, 0.125, 0.0).astype(BF16)
    middle = dot2(split(jnp.concatenate(halves, axis=1)), pool)
    me_[0, mown] = middle.reshape(mx, R, bz)
    if fused:
        lanes = []
        for i in range(cx):
            total = None
            for a in range(4):
                for b in range(4):
                    part = fe[R + 4 * i + a, pl.ds(R + b, cy, stride=4), :]
                    total = part if total is None else total + part
            lanes.append(total)
        row, col = iota((cx * bz, bz), 0), iota((cx * bz, bz), 1)
        pool = jnp.where(jnp.right_shift(row, 2) == col, 1.0 / 64.0, 0.0).astype(BF16)
        ga[iy, ix, iz] = dot2(split(jnp.concatenate(lanes, axis=1)), pool)
    pl.semaphore_wait(barrier, greetings)
    for copy in gather[2] + mid_x + mid_y + y_halo + x_halo:
        copy.start()

    for copy in mid_x:
        copy.wait_recv()
    for copy in mid_c:
        copy.start()
    for copy in gather[2]:
        copy.wait_recv()
    for copy in gather[0]:
        copy.start()
    for copy in y_halo:
        copy.wait_recv()
    for copy in corner:
        copy.start()

    def taps_of(level, k):
        return [taps[level * TERMS + k, t] for t in range(R + 1)]

    for copy in x_halo:
        copy.wait_recv()

    def x_filter(load, store, level, tiles, length):
        @pl.loop(0, length)
        def _(i):
            g = [taps_of(level, k) for k in range(TERMS)]
            for tile in tiles:
                centre = load(i + R, tile)
                totals = [g[k][0] * centre for k in range(TERMS)]
                for t in range(1, R + 1):
                    pair = load(i + R - t, tile) + load(i + R + t, tile)
                    totals = [totals[k] + g[k][t] * pair for k in range(TERMS)]
                for k in range(TERMS):
                    store(k, i, tile, totals[k])

    def load_f(i, tile):
        return fe[i, tile * 8:tile * 8 + 8, :]

    def store_f(k, i, tile, value):
        x1[k, i, tile * 8:tile * 8 + 8, :] = value

    last = (by + R) // 8
    x_filter(load_f, store_f, 0, range(1, last), bx)

    for copy in mid_y + mid_c:
        copy.wait_recv()
    slots = range(high + 1)

    def load_m(i, slot):
        return me_[slot, i]

    def store_m(k, i, slot, value):
        m1[slot, k, i] = value

    x_filter(load_m, store_m, 1, slots, mx)
    low_lanes = iota((R, bz), 1) < mz

    @pl.loop(0, mx // 2)
    def _(i):
        for k in range(TERMS):
            g = taps_of(1, k)
            parts = []
            for s in range(2):
                own, low, top_ = m1[0, k, 2 * i + s], m1[1, k, 2 * i + s], m1[high, k, 2 * i + s]
                bet[s, 0:8] = pltpu.roll(jnp.where(low_lanes, own, low), mz, 1)
                bet[s, 8:16] = own
                bet[s, 16:24] = pltpu.roll(jnp.where(low_lanes, top_, own), mz, 1)
                total = g[0] * own
                for t in range(1, R + 1):
                    total = total + g[t] * (bet[s, 8 - t:16 - t, :] + bet[s, 8 + t:16 + t, :])
                parts.append(total)
            hi, lo = split(jnp.concatenate(parts, axis=0))
            rows = pl.ds(pl.multiple_of(i * 16, 16), 16)
            mh[rows, k * bz:(k + 1) * bz] = hi
            ml[rows, k * bz:(k + 1) * bz] = lo

    mid = (mh[...], ml[...])
    edge = dot3(weights_edge[1], mid, NT)
    zem[...] = jnp.concatenate([edge[0:2 * R], edge[2 * R:4 * R]], axis=1)
    for copy in z_mid:
        copy.start()
    between = [dot3(mid, (t_hi[1 + half], t_lo[1 + half])) for half in range(2)]
    for copy in gather[0]:
        copy.wait_recv()
    for copy in gather[1]:
        copy.start()

    for copy in corner:
        copy.wait_recv()
    x_filter(load_f, store_f, 0, (0, last), bx)

    @pl.loop(0, bx)
    def _(i):
        for k in range(TERMS):
            g = taps_of(0, k)
            for pair in range(by // 16):
                base = R + pair * 16
                parts = []
                for s in range(2):
                    at = base + 8 * s
                    total = g[0] * x1[k, i, at:at + 8, :]
                    for t in range(1, R + 1):
                        total = total + g[t] * (
                            x1[k, i, at - t:at - t + 8, :] + x1[k, i, at + t:at + t + 8, :]
                        )
                    parts.append(total)
                hi, lo = split(jnp.concatenate(parts, axis=0))
                rows = pl.ds(pl.multiple_of(i * by + pair * 16, 16), 16)
                ph[rows, k * bz:(k + 1) * bz] = hi
                pl_[rows, k * bz:(k + 1) * bz] = lo

    fine = (ph[...], pl_[...])
    ze[...] = dot3(weights_edge[0], fine, NT)
    for copy in z_edge:
        copy.start()
    near = dot3(fine, (t_hi[0], t_lo[0]))
    out[...] = near.reshape(bx, by, bz)

    if fused:
        for copy in local[1:]:
            copy.wait()

        for copy in gather[1]:
            copy.wait_recv()

        group = jnp.right_shift(iota((ngx * ngy * cy, bz), 1), cz.bit_length() - 1)
        blocks = [ga[:, :, j].reshape(ngx * ngy * cy, bz) for j in range(ngz)]
        lines = []
        for i in range(cx):
            line = None
            for j in range(ngz):
                shift = (j * cz - i * cz) % bz
                moved = pltpu.roll(blocks[j], shift, 1) if shift else blocks[j]
                line = moved if line is None else jnp.where(group == j, moved, line)
            lines.append(line)
        lines = jnp.concatenate(lines, axis=0)
        modes = dot3(split(lines), split(qz_v[...]))
        modes = dot3(split(fwd_v[...]), split(modes)) * mult_v[...]
        modes = dot3(split(inv_v[...]), split(modes))
        distant = dot3(split(modes), split(spr_v[...]))
        for i in range(cx):
            part = distant[i * cy:(i + 1) * cy]
            dis[i, pl.ds(0, cy, stride=2), :] = part
            dis[i, pl.ds(1, cy, stride=2), :] = part

    for copy in z_mid:
        copy.wait_recv()
    row, col = iota((2 * R, bz), 0), iota((2 * R, bz), 1)
    place = jnp.where(row < R, row + bz - R, row - R) == col
    place = jnp.where(place, 1.0, 0.0).astype(BF16)
    spread = jnp.where(row < R, row + mz - R, row - R) == jnp.right_shift(col, 1)
    spread = jnp.where(spread, 1.0, 0.0).astype(BF16)
    edge = dot2(split(zrm[...].T), spread)
    for half in range(2):
        for i in range(mx):
            at = i * R
            value = between[half][at:at + R] + edge[half * mx * R + at:half * mx * R + at + R]
            if fused:
                value = value + dis[i // 2, half * R:half * R + R, :]
            up[i, pl.ds(2 * R * half, R, stride=2), :] = value
            up[i, pl.ds(2 * R * half + 1, R, stride=2), :] = value
    for copy in z_edge:
        copy.wait_recv()
    edge = dot2(split(zr[...].T), place)
    for i in range(bx):
        out[i] = out[i] + (edge[i * by:(i + 1) * by] + up[i // 2])

    for copy in x_halo + y_halo + corner + mid_x + mid_y + mid_c + z_mid + z_edge + sum(gather, []):
        copy.wait_send()


def expand(field):
    return jnp.repeat(jnp.repeat(jnp.repeat(field, 2, axis=0), 2, axis=1), 2, axis=2)


def coarse_of(field):
    s = field.shape
    return field.reshape(s[0] // 4, 4, s[1] // 4, 4, s[2] // 4, 4).mean(axis=(1, 3, 5))


def turn(real, imag, cosine, sine, form, sign):
    ein = functools.partial(jnp.einsum, form, precision=HIGHEST)
    return (
        ein(cosine, real) + sign * ein(sine, imag),
        ein(cosine, imag) - sign * ein(sine, real),
    )


def dft(count):
    modes = np.arange(count)
    angle = 2.0 * np.pi * (modes[:, None] * modes[None, :] % count) / count
    return jnp.asarray(np.cos(angle), F32), jnp.asarray(np.sin(angle), F32)


def solve_top(coarse, sizes):
    bx, by, bz = coarse.shape
    nx, ny, nz = bx * sizes[0], by * sizes[1], bz * sizes[2]
    a2a = functools.partial(lax.all_to_all, tiled=True)
    column = lax.all_gather(coarse, "gx", axis=0, tiled=True)
    tx, ty, tz = dft(nx), dft(ny), dft(nz)
    real, imag = turn(column, jnp.zeros_like(column), *tx, "mx,xyz->myz", 1.0)
    pencil = a2a(jnp.stack([real, imag]), "gy", split_axis=1, concat_axis=2)
    pencil = a2a(pencil, "gz", split_axis=1, concat_axis=3)
    real, imag = turn(pencil[0], pencil[1], *ty, "my,xyz->xmz", 1.0)
    real, imag = turn(real, imag, *tz, "mz,xyz->xym", 1.0)
    rows_y = nx // sizes[1]
    rows = rows_y // sizes[2]
    start = lax.axis_index("gy") * rows_y + lax.axis_index("gz") * rows
    lam_x = jnp.asarray(lam_of(np.arange(nx), nx), F32)
    lam = (
        lax.dynamic_slice_in_dim(lam_x, start, rows, 0)[:, None, None]
        + jnp.asarray(lam_of(np.arange(ny), ny), F32)[None, :, None]
        + jnp.asarray(lam_of(np.arange(nz), nz), F32)[None, None, :]
    )
    mult = jnp.where(lam <= 0.0, 0.0, strength * jnp.exp(-lam) / (lam + screening))
    real, imag = turn(real * mult, imag * mult, *tz, "mz,xyz->xym", -1.0)
    back = a2a(jnp.stack([real, imag]), "gz", split_axis=3, concat_axis=1)
    real, imag = turn(back[0], back[1], *ty, "my,xyz->xmz", -1.0)
    back = a2a(jnp.stack([real, imag]), "gy", split_axis=2, concat_axis=1)
    whole, _ = turn(back[0], back[1], *tx, "mx,xyz->myz", -1.0)
    whole = whole / float(nx * ny * nz)
    return lax.dynamic_slice_in_dim(whole, lax.axis_index("gx") * bx, bx, 0)


def shards(sizes, charges, width, weight):
    bx, by, bz = block = charges.shape
    mx, my = bx // 2, by // 2
    cx, cy, cz = coarse = (bx // 4, by // 4, bz // 4)
    ngx, ngy, ngz = sizes
    count = ngx * ngy * ngz
    points = ngx * cx * ngy * cy
    fused = points <= 512 and ngz * cz == bz and count <= 64
    vmem = pltpu.VMEM
    slots = 2 if ngy == 2 else 3
    scratch = [
        vmem((bx + 2 * R, by + 2 * R, bz), F32),
        vmem((TERMS, bx, by + 2 * R, bz), F32),
        vmem((bx * by, TERMS * bz), BF16),
        vmem((bx * by, TERMS * bz), BF16),
        vmem((slots, mx + 2 * R, R, bz), F32),
        vmem((slots, TERMS, mx, R, bz), F32),
        vmem((mx * R, TERMS * bz), BF16),
        vmem((mx * R, TERMS * bz), BF16),
        vmem((2 * R, bx * by), F32),
        vmem((2 * R, bx * by), F32),
        vmem((2 * R, 2 * mx * R), F32),
        vmem((2 * R, 2 * mx * R), F32),
        vmem((3, TERMS * bz, bz), BF16),
        vmem((3, TERMS * bz, bz), BF16),
        vmem((2 * TERMS, R + 1, 8, 128), F32),
        vmem((2, 3 * R, bz), F32),
        vmem((mx, by, bz), F32),
        vmem((cx, my, bz), F32),
        pltpu.SemaphoreType.DMA((20,)),
        pltpu.SemaphoreType.DMA((20,)),
        pltpu.SemaphoreType.DMA((6,)),
    ]
    operands = [charges, width, weight]
    anywhere = pl.BlockSpec(memory_space=pl.ANY)
    small = pl.BlockSpec(memory_space=pltpu.SMEM)
    specs = [anywhere, small, small]
    if fused:
        tables = top_tables(sizes, coarse)
        operands += [jnp.asarray(t) for t in tables]
        specs += [anywhere] * len(tables)
        scratch += [
            vmem((ngy, ngx, ngz, cy, cx * cz), F32),
            vmem(tables[0].shape, F32),
            vmem(tables[1].shape, F32),
            vmem(tables[2].shape, F32),
            vmem(tables[3].shape[1:], F32),
            vmem(tables[4].shape[1:], F32),
            pltpu.SemaphoreType.DMA((ngx + ngy + ngz - 3,)),
            pltpu.SemaphoreType.DMA((ngx + ngy + ngz - 3,)),
        ]
    result = pl.pallas_call(
        functools.partial(body, sizes, block, fused),
        out_shape=pltpu.VMEM(block, F32),
        in_specs=specs,
        out_specs=pl.BlockSpec(memory_space=pltpu.VMEM),
        scratch_shapes=scratch,
        compiler_params=pltpu.CompilerParams(collective_id=0, has_side_effects=True),
    )(*operands)
    if not fused:
        result = result + expand(expand(solve_top(coarse_of(charges), sizes)))
    return result


def solution(mesh):
    sizes = tuple(mesh.shape[a] for a in AXES)
    placed = (P(*AXES), P(), P())
    return jax.shard_map(
        functools.partial(shards, sizes), mesh=mesh, in_specs=placed, out_specs=P(*AXES),
        check_vma=False,
    )
```

```python
import functools
import math

import jax
import jax.numpy as jnp
import numpy as np
from jax import lax
from jax.experimental import pallas as pl
from jax.experimental.pallas import tpu as pltpu
from jax.sharding import PartitionSpec as P

TERMS = 4
R = 8
HIGHEST = lax.Precision.HIGHEST
screening = 0.01
strength = 4.0
AXES = ("gx", "gy", "gz")
MESH = pl.DeviceIdType.MESH
F32 = jnp.float32
BF16 = jnp.bfloat16


def real_basis(count):
    points = np.arange(count)
    rows, freqs = [], []
    for m in range(count // 2 + 1):
        angle = 2.0 * np.pi * ((m * points) % count) / count
        single = m == 0 or 2 * m == count
        scale = math.sqrt((1.0 if single else 2.0) / count)
        rows.append(scale * np.cos(angle))
        freqs.append(m)
        if not single:
            rows.append(scale * np.sin(angle))
            freqs.append(m)
    return np.stack(rows), np.array(freqs)


def lam_of(freqs, count):
    return 2.0 - 2.0 * np.cos(2.0 * np.pi * freqs / count)


def top_tables(sizes, block):
    ngx, ngy, ngz = sizes
    cx, cy, cz = block
    nx, ny, nz = ngx * cx, ngy * cy, ngz * cz
    (qx, fx), (qy, fy), (qz, fz) = real_basis(nx), real_basis(ny), real_basis(nz)
    lam = (
        lam_of(fx, nx)[:, None, None] + lam_of(fy, ny)[None, :, None] + lam_of(fz, nz)[None, None, :]
    )
    zero = (fx[:, None, None] + fy[None, :, None] + fz[None, None, :]) == 0
    mult = np.where(zero, 0.0, strength * np.exp(-lam) / (lam + screening)).reshape(nx * ny, nz)
    kron = np.kron(qx, qy).reshape(nx * ny, ngx, cx, ngy, cy)
    forward = kron.transpose(0, 2, 3, 1, 4).reshape(nx * ny, nx * ny)
    inverse = kron.transpose(1, 3, 2, 4, 0).reshape(ngx * ngy, cx * cy, nx * ny)
    spread = np.repeat(qz, 4, axis=1).reshape(nz, ngz, 4 * cz).transpose(1, 0, 2)
    return [np.asarray(t, np.float32) for t in (qz.T, forward, mult, inverse, spread)]


def split(value):
    high = value.astype(BF16)
    return high, (value - high.astype(F32)).astype(BF16)


NN = (((1,), (0,)), ((), ()))
NT = (((1,), (1,)), ((), ()))


def mm(a, b, dims=NN):
    return lax.dot_general(a, b, dims, preferred_element_type=F32)


def dot3(a, b, dims=NN):
    (ah, al), (bh, bl) = a, b
    return mm(ah, bh, dims) + (mm(al, bh, dims) + mm(ah, bl, dims))


def dot2(a, exact):
    return mm(a[0], exact) + mm(a[1], exact)


def iota(shape, dim):
    return lax.broadcasted_iota(jnp.int32, shape, dim)


def body(sizes, block, fused, *refs):
    ngx, ngy, ngz = sizes
    bx, by, bz = block
    mx, my, mz = bx // 2, by // 2, bz // 2
    cx, cy, cz = bx // 4, by // 4, bz // 4
    if fused:
        (charges, width, weight, qz_h, fwd_h, mult_h, inv_h, spr_h, out) = refs[:9]
        refs = refs[9:]
    else:
        (charges, width, weight, out) = refs[:4]
        refs = refs[4:]
    (fe, x1, ph, pl_, me_, m1, mh, ml, ze, zr, zem, zrm, t_hi, t_lo, taps, bet, up, dis, ssem, rsem, lsem) = refs[:21]
    if fused:
        (ga, qz_v, fwd_v, mult_v, inv_v, spr_v, gs, gr) = refs[21:]

    ix, iy, iz = (lax.axis_index(a) for a in AXES)

    def step(axis, by_):
        position = [ix, iy, iz]
        n = sizes[axis]
        position[axis] = lax.rem(position[axis] + by_ + n, n)
        return tuple(position)

    barrier = pltpu.get_barrier_semaphore()
    greetings = 0
    for axis in range(3):
        n = sizes[axis]
        for off in range(1, n) if fused else ((1, -1) if n > 2 else (1,)):
            pl.semaphore_signal(barrier, 1, device_id=step(axis, off), device_id_type=MESH)
            greetings += 1

    local = [pltpu.make_async_copy(charges, fe.at[R:R + bx, R:R + by], lsem.at[0])]
    if fused:
        local += [
            pltpu.make_async_copy(qz_h, qz_v, lsem.at[1]),
            pltpu.make_async_copy(fwd_h, fwd_v, lsem.at[2]),
            pltpu.make_async_copy(mult_h, mult_v, lsem.at[3]),
            pltpu.make_async_copy(inv_h.at[ix * ngy + iy], inv_v, lsem.at[4]),
            pltpu.make_async_copy(spr_h.at[iz], spr_v, lsem.at[5]),
        ]
    for copy in local:
        copy.start()

    def remote(src, dst, slot, target):
        return pltpu.make_async_remote_copy(
            src_ref=src, dst_ref=dst, send_sem=ssem.at[slot], recv_sem=rsem.at[slot],
            device_id=target, device_id_type=MESH,
        )

    xp, xm, yp, ym, zp, zm = step(0, 1), step(0, -1), step(1, 1), step(1, -1), step(2, 1), step(2, -1)
    lo_x, hi_x, lo_y, hi_y = slice(0, R), slice(R + bx, 2 * R + bx), slice(0, R), slice(R + by, 2 * R + by)
    own_x, own_y = slice(R, R + bx), slice(R, R + by)
    x_halo = [
        remote(charges.at[bx - R:bx], fe.at[lo_x, own_y], 0, xp),
        remote(charges.at[0:R], fe.at[hi_x, own_y], 1, xm),
    ]
    y_halo = [
        remote(charges.at[:, by - R:by], fe.at[own_x, lo_y], 2, yp),
        remote(charges.at[:, 0:R], fe.at[own_x, hi_y], 3, ym),
    ]
    corner = [
        remote(fe.at[bx:bx + R, lo_y], fe.at[lo_x, lo_y], 4, xp),
        remote(fe.at[bx:bx + R, hi_y], fe.at[lo_x, hi_y], 5, xp),
        remote(fe.at[R:2 * R, lo_y], fe.at[hi_x, lo_y], 6, xm),
        remote(fe.at[R:2 * R, hi_y], fe.at[hi_x, hi_y], 7, xm),
    ]
    mown, mlo, mhi = slice(R, R + mx), slice(0, R), slice(R + mx, 2 * R + mx)
    mid_x = [
        remote(me_.at[0, mx:R + mx], me_.at[0, mlo], 8, xp),
        remote(me_.at[0, R:2 * R], me_.at[0, mhi], 9, xm),
    ]
    mid_y = [remote(me_.at[0, mown], me_.at[1, mown], 10, yp)]
    mid_c = [
        remote(me_.at[0, mlo], me_.at[1, mlo], 12, yp),
        remote(me_.at[0, mhi], me_.at[1, mhi], 13, yp),
    ]
    high = 1
    if ngy > 2:
        high = 2
        mid_y.append(remote(me_.at[0, mown], me_.at[2, mown], 11, ym))
        mid_c.append(remote(me_.at[0, mlo], me_.at[2, mlo], 14, ym))
        mid_c.append(remote(me_.at[0, mhi], me_.at[2, mhi], 15, ym))
    z_edge = [
        remote(ze.at[0:R], zr.at[0:R], 16, zm),
        remote(ze.at[R:2 * R], zr.at[R:2 * R], 17, zp),
    ]
    z_mid = [
        remote(zem.at[0:R], zrm.at[0:R], 18, zm),
        remote(zem.at[R:2 * R], zrm.at[R:2 * R], 19, zp),
    ]

    gather = [[], [], []]
    if fused:
        slot = 0
        for axis, part in ((2, ga.at[iy, ix, iz]), (0, ga.at[iy, ix]), (1, ga.at[iy])):
            for off in range(1, sizes[axis]):
                gather[axis].append(pltpu.make_async_remote_copy(
                    src_ref=part, dst_ref=part, send_sem=gs.at[slot], recv_sem=gr.at[slot],
                    device_id=step(axis, off), device_id_type=MESH,
                ))
                slot += 1

    weights_edge = []
    for level in range(2):
        edges = []
        for k in range(TERMS):
            sigma = jnp.full((1, 128), width[level, k], F32)
            rate = 1.0 / (2.0 * sigma * sigma)
            values = [jnp.exp(-(float(t * t) * rate)) for t in range(R + 1)]
            total = values[0]
            for t in range(1, R + 1):
                total = total + 2.0 * values[t]
            inverse = 1.0 / total
            for t in range(R + 1):
                taps[level * TERMS + k, t] = jnp.broadcast_to(values[t] * inverse, (8, 128))
            scale = inverse * weight[level, k]

            def band(d, keep):
                d = d.astype(F32)
                inside = jnp.abs(d) <= float(R)
                if keep is not None:
                    inside = jnp.logical_and(inside, keep)
                return jnp.where(inside, jnp.exp(-(d * d * rate)) * scale, 0.0)

            if level == 0:
                shape = (bz, bz)
                hi, lo = split(band(iota(shape, 0) - iota(shape, 1), None))
                t_hi[0, k * bz:(k + 1) * bz] = hi
                t_lo[0, k * bz:(k + 1) * bz] = lo
                shape = (2 * R, bz)
                row, z = iota(shape, 0), iota(shape, 1)
                edges.append(band(z - jnp.where(row < R, row - R, row - R + bz), None))
            else:
                shape = (bz, bz)
                row = iota(shape, 0)
                for half in range(2):
                    keep = jnp.right_shift(row, mz.bit_length() - 1) == half
                    hi, lo = split(band((row - half * mz) - jnp.right_shift(iota(shape, 1), 1), keep))
                    t_hi[1 + half, k * bz:(k + 1) * bz] = hi
                    t_lo[1 + half, k * bz:(k + 1) * bz] = lo
                shape = (2 * R, bz)
                row, z = iota(shape, 0), iota(shape, 1)
                target = jnp.where(row < R, row - R, row - R + mz)
                pair = [
                    band(z - half * mz - target, jnp.right_shift(z, mz.bit_length() - 1) == half)
                    for half in range(2)
                ]
                edges.append(jnp.concatenate(pair, axis=0))
        weights_edge.append(split(jnp.concatenate(edges, axis=1)))

    local[0].wait()
    halves = []
    for half in range(2):
        rows = []
        for i in range(mx):
            total = None
            for a in range(2):
                for b in range(2):
                    part = fe[R + 2 * i + a, pl.ds(R + half * my + b, R, stride=2), :]
                    total = part if total is None else total + part
            rows.append(total)
        halves.append(jnp.concatenate(rows, axis=0))
    row, col = iota((2 * bz, bz), 0), iota((2 * bz, bz), 1)
    pool = jnp.where(jnp.right_shift(row, 1) == col, 0.125, 0.0).astype(BF16)
    middle = dot2(split(jnp.concatenate(halves, axis=1)), pool)
    me_[0, mown] = middle.reshape(mx, R, bz)
    if fused:
        lanes = []
        for i in range(cx):
            total = None
            for a in range(4):
                for b in range(4):
                    part = fe[R + 4 * i + a, pl.ds(R + b, cy, stride=4), :]
                    total = part if total is None else total + part
            lanes.append(total)
        row, col = iota((cx * bz, bz), 0), iota((cx * bz, bz), 1)
        pool = jnp.where(jnp.right_shift(row, 2) == col, 1.0 / 64.0, 0.0).astype(BF16)
        ga[iy, ix, iz] = dot2(split(jnp.concatenate(lanes, axis=1)), pool)
    pl.semaphore_wait(barrier, greetings)
    for copy in gather[2] + mid_x + y_halo + x_halo + mid_y:
        copy.start()

    for copy in mid_x:
        copy.wait_recv()
    for copy in mid_c:
        copy.start()
    for copy in gather[2]:
        copy.wait_recv()
    for copy in gather[0]:
        copy.start()
    for copy in y_halo:
        copy.wait_recv()
    for copy in corner:
        copy.start()

    def taps_of(level, k):
        return [taps[level * TERMS + k, t] for t in range(R + 1)]

    for copy in x_halo:
        copy.wait_recv()

    def x_filter(load, store, level, tiles, length):
        @pl.loop(0, length)
        def _(i):
            g = [taps_of(level, k) for k in range(TERMS)]
            for tile in tiles:
                centre = load(i + R, tile)
                totals = [g[k][0] * centre for k in range(TERMS)]
                for t in range(1, R + 1):
                    pair = load(i + R - t, tile) + load(i + R + t, tile)
                    totals = [totals[k] + g[k][t] * pair for k in range(TERMS)]
                for k in range(TERMS):
                    store(k, i, tile, totals[k])

    def load_f(i, tile):
        return fe[i, tile * 8:tile * 8 + 8, :]

    def store_f(k, i, tile, value):
        x1[k, i, tile * 8:tile * 8 + 8, :] = value

    last = (by + R) // 8
    x_filter(load_f, store_f, 0, range(1, last), bx)

    for copy in mid_y + mid_c:
        copy.wait_recv()
    slots = range(high + 1)

    def load_m(i, slot):
        return me_[slot, i]

    def store_m(k, i, slot, value):
        m1[slot, k, i] = value

    x_filter(load_m, store_m, 1, slots, mx)
    low_lanes = iota((R, bz), 1) < mz

    @pl.loop(0, mx // 2)
    def _(i):
        for k in range(TERMS):
            g = taps_of(1, k)
            parts = []
            for s in range(2):
                own, low, top_ = m1[0, k, 2 * i + s], m1[1, k, 2 * i + s], m1[high, k, 2 * i + s]
                bet[s, 0:8] = pltpu.roll(jnp.where(low_lanes, own, low), mz, 1)
                bet[s, 8:16] = own
                bet[s, 16:24] = pltpu.roll(jnp.where(low_lanes, top_, own), mz, 1)
                total = g[0] * own
                for t in range(1, R + 1):
                    total = total + g[t] * (bet[s, 8 - t:16 - t, :] + bet[s, 8 + t:16 + t, :])
                parts.append(total)
            hi, lo = split(jnp.concatenate(parts, axis=0))
            rows = pl.ds(pl.multiple_of(i * 16, 16), 16)
            mh[rows, k * bz:(k + 1) * bz] = hi
            ml[rows, k * bz:(k + 1) * bz] = lo

    mid = (mh[...], ml[...])
    edge = dot3(weights_edge[1], mid, NT)
    zem[...] = jnp.concatenate([edge[0:2 * R], edge[2 * R:4 * R]], axis=1)
    for copy in z_mid:
        copy.start()
    between = [dot3(mid, (t_hi[1 + half], t_lo[1 + half])) for half in range(2)]
    for copy in gather[0]:
        copy.wait_recv()
    for copy in gather[1]:
        copy.start()

    for copy in corner:
        copy.wait_recv()
    x_filter(load_f, store_f, 0, (0, last), bx)

    @pl.loop(0, bx)
    def _(i):
        for k in range(TERMS):
            g = taps_of(0, k)
            for pair in range(by // 16):
                base = R + pair * 16
                parts = []
                for s in range(2):
                    at = base + 8 * s
                    total = g[0] * x1[k, i, at:at + 8, :]
                    for t in range(1, R + 1):
                        total = total + g[t] * (
                            x1[k, i, at - t:at - t + 8, :] + x1[k, i, at + t:at + t + 8, :]
                        )
                    parts.append(total)
                hi, lo = split(jnp.concatenate(parts, axis=0))
                rows = pl.ds(pl.multiple_of(i * by + pair * 16, 16), 16)
                ph[rows, k * bz:(k + 1) * bz] = hi
                pl_[rows, k * bz:(k + 1) * bz] = lo

    fine = (ph[...], pl_[...])
    ze[...] = dot3(weights_edge[0], fine, NT)
    for copy in z_edge:
        copy.start()
    near = dot3(fine, (t_hi[0], t_lo[0]))
    out[...] = near.reshape(bx, by, bz)

    if fused:
        for copy in local[1:]:
            copy.wait()

        for copy in gather[1]:
            copy.wait_recv()

        group = jnp.right_shift(iota((ngx * ngy * cy, bz), 1), cz.bit_length() - 1)
        blocks = [ga[:, :, j].reshape(ngx * ngy * cy, bz) for j in range(ngz)]
        lines = []
        for i in range(cx):
            line = None
            for j in range(ngz):
                shift = (j * cz - i * cz) % bz
                moved = pltpu.roll(blocks[j], shift, 1) if shift else blocks[j]
                line = moved if line is None else jnp.where(group == j, moved, line)
            lines.append(line)
        lines = jnp.concatenate(lines, axis=0)
        modes = dot3(split(lines), split(qz_v[...]))
        modes = dot3(split(fwd_v[...]), split(modes)) * mult_v[...]
        modes = dot3(split(inv_v[...]), split(modes))
        distant = dot3(split(modes), split(spr_v[...]))
        for i in range(cx):
            part = distant[i * cy:(i + 1) * cy]
            dis[i, pl.ds(0, cy, stride=2), :] = part
            dis[i, pl.ds(1, cy, stride=2), :] = part

    for copy in z_mid:
        copy.wait_recv()
    row, col = iota((2 * R, bz), 0), iota((2 * R, bz), 1)
    place = jnp.where(row < R, row + bz - R, row - R) == col
    place = jnp.where(place, 1.0, 0.0).astype(BF16)
    spread = jnp.where(row < R, row + mz - R, row - R) == jnp.right_shift(col, 1)
    spread = jnp.where(spread, 1.0, 0.0).astype(BF16)
    edge = dot2(split(zrm[...].T), spread)
    for half in range(2):
        for i in range(mx):
            at = i * R
            value = between[half][at:at + R] + edge[half * mx * R + at:half * mx * R + at + R]
            if fused:
                value = value + dis[i // 2, half * R:half * R + R, :]
            up[i, pl.ds(2 * R * half, R, stride=2), :] = value
            up[i, pl.ds(2 * R * half + 1, R, stride=2), :] = value
    for copy in z_edge:
        copy.wait_recv()
    edge = dot2(split(zr[...].T), place)
    for i in range(bx):
        out[i] = out[i] + (edge[i * by:(i + 1) * by] + up[i // 2])

    for copy in x_halo + y_halo + corner + mid_x + mid_y + mid_c + z_mid + z_edge + sum(gather, []):
        copy.wait_send()


def expand(field):
    return jnp.repeat(jnp.repeat(jnp.repeat(field, 2, axis=0), 2, axis=1), 2, axis=2)


def coarse_of(field):
    s = field.shape
    return field.reshape(s[0] // 4, 4, s[1] // 4, 4, s[2] // 4, 4).mean(axis=(1, 3, 5))


def turn(real, imag, cosine, sine, form, sign):
    ein = functools.partial(jnp.einsum, form, precision=HIGHEST)
    return (
        ein(cosine, real) + sign * ein(sine, imag),
        ein(cosine, imag) - sign * ein(sine, real),
    )


def dft(count):
    modes = np.arange(count)
    angle = 2.0 * np.pi * (modes[:, None] * modes[None, :] % count) / count
    return jnp.asarray(np.cos(angle), F32), jnp.asarray(np.sin(angle), F32)


def solve_top(coarse, sizes):
    bx, by, bz = coarse.shape
    nx, ny, nz = bx * sizes[0], by * sizes[1], bz * sizes[2]
    a2a = functools.partial(lax.all_to_all, tiled=True)
    column = lax.all_gather(coarse, "gx", axis=0, tiled=True)
    tx, ty, tz = dft(nx), dft(ny), dft(nz)
    real, imag = turn(column, jnp.zeros_like(column), *tx, "mx,xyz->myz", 1.0)
    pencil = a2a(jnp.stack([real, imag]), "gy", split_axis=1, concat_axis=2)
    pencil = a2a(pencil, "gz", split_axis=1, concat_axis=3)
    real, imag = turn(pencil[0], pencil[1], *ty, "my,xyz->xmz", 1.0)
    real, imag = turn(real, imag, *tz, "mz,xyz->xym", 1.0)
    rows_y = nx // sizes[1]
    rows = rows_y // sizes[2]
    start = lax.axis_index("gy") * rows_y + lax.axis_index("gz") * rows
    lam_x = jnp.asarray(lam_of(np.arange(nx), nx), F32)
    lam = (
        lax.dynamic_slice_in_dim(lam_x, start, rows, 0)[:, None, None]
        + jnp.asarray(lam_of(np.arange(ny), ny), F32)[None, :, None]
        + jnp.asarray(lam_of(np.arange(nz), nz), F32)[None, None, :]
    )
    mult = jnp.where(lam <= 0.0, 0.0, strength * jnp.exp(-lam) / (lam + screening))
    real, imag = turn(real * mult, imag * mult, *tz, "mz,xyz->xym", -1.0)
    back = a2a(jnp.stack([real, imag]), "gz", split_axis=3, concat_axis=1)
    real, imag = turn(back[0], back[1], *ty, "my,xyz->xmz", -1.0)
    back = a2a(jnp.stack([real, imag]), "gy", split_axis=2, concat_axis=1)
    whole, _ = turn(back[0], back[1], *tx, "mx,xyz->myz", -1.0)
    whole = whole / float(nx * ny * nz)
    return lax.dynamic_slice_in_dim(whole, lax.axis_index("gx") * bx, bx, 0)


def shards(sizes, charges, width, weight):
    bx, by, bz = block = charges.shape
    mx, my = bx // 2, by // 2
    cx, cy, cz = coarse = (bx // 4, by // 4, bz // 4)
    ngx, ngy, ngz = sizes
    count = ngx * ngy * ngz
    points = ngx * cx * ngy * cy
    fused = points <= 512 and ngz * cz == bz and count <= 64
    vmem = pltpu.VMEM
    slots = 2 if ngy == 2 else 3
    scratch = [
        vmem((bx + 2 * R, by + 2 * R, bz), F32),
        vmem((TERMS, bx, by + 2 * R, bz), F32),
        vmem((bx * by, TERMS * bz), BF16),
        vmem((bx * by, TERMS * bz), BF16),
        vmem((slots, mx + 2 * R, R, bz), F32),
        vmem((slots, TERMS, mx, R, bz), F32),
        vmem((mx * R, TERMS * bz), BF16),
        vmem((mx * R, TERMS * bz), BF16),
        vmem((2 * R, bx * by), F32),
        vmem((2 * R, bx * by), F32),
        vmem((2 * R, 2 * mx * R), F32),
        vmem((2 * R, 2 * mx * R), F32),
        vmem((3, TERMS * bz, bz), BF16),
        vmem((3, TERMS * bz, bz), BF16),
        vmem((2 * TERMS, R + 1, 8, 128), F32),
        vmem((2, 3 * R, bz), F32),
        vmem((mx, by, bz), F32),
        vmem((cx, my, bz), F32),
        pltpu.SemaphoreType.DMA((20,)),
        pltpu.SemaphoreType.DMA((20,)),
        pltpu.SemaphoreType.DMA((6,)),
    ]
    operands = [charges, width, weight]
    anywhere = pl.BlockSpec(memory_space=pl.ANY)
    small = pl.BlockSpec(memory_space=pltpu.SMEM)
    specs = [anywhere, small, small]
    if fused:
        tables = top_tables(sizes, coarse)
        operands += [jnp.asarray(t) for t in tables]
        specs += [anywhere] * len(tables)
        scratch += [
            vmem((ngy, ngx, ngz, cy, cx * cz), F32),
            vmem(tables[0].shape, F32),
            vmem(tables[1].shape, F32),
            vmem(tables[2].shape, F32),
            vmem(tables[3].shape[1:], F32),
            vmem(tables[4].shape[1:], F32),
            pltpu.SemaphoreType.DMA((ngx + ngy + ngz - 3,)),
            pltpu.SemaphoreType.DMA((ngx + ngy + ngz - 3,)),
        ]
    result = pl.pallas_call(
        functools.partial(body, sizes, block, fused),
        out_shape=pltpu.VMEM(block, F32),
        in_specs=specs,
        out_specs=pl.BlockSpec(memory_space=pltpu.VMEM),
        scratch_shapes=scratch,
        compiler_params=pltpu.CompilerParams(collective_id=0, has_side_effects=True),
    )(*operands)
    if not fused:
        result = result + expand(expand(solve_top(coarse_of(charges), sizes)))
    return result


def solution(mesh):
    sizes = tuple(mesh.shape[a] for a in AXES)
    placed = (P(*AXES), P(), P())
    return jax.shard_map(
        functools.partial(shards, sizes), mesh=mesh, in_specs=placed, out_specs=P(*AXES),
        check_vma=False,
    )
```
